256 devices in a mesh: row: 4 (over x_lo, core), col: 16 (over z, x_hi), layer: 4 (over y).
Axes of the slice: x: 4 (x_hi: 2, x_lo: 2; x = x_hi * 2 + x_lo), y: 4, z: 8, core: 2. Of those that a mesh axis runs over, the one named last changes fastest.
Arguments:
- values: bfloat16 [8192, 8192], P('row', 'col'), may hold values from 0.0099487305 to 1
- tile_mask: int32 [64, 64], P('row', 'col'), may hold values from 0 to 1, as said below
Outputs:
- clustered: float32 [8192, 8192], P('row', ('col', 'layer'))
The draws below stay inside these ranges and needn't reach their ends.
Inputs may be any that keep to these rules, and one draw needn't show every extreme that they name: `tile_mask`: every diagonal tile is nonzero. The blocks of (64 / 4) x 4 tiles that one device holds each have at most 32 nonzero tiles and at least 4; the block in the first grid row and first grid column has exactly 32.
All inputs are finite; a program needn't handle non-finite values.
Results may differ from the reference program's by a relative error of at most 0.0065.
Values may be sent and summed in bfloat16 or wider, within the bound.
No kernel may reach another device: no remote copies, remote signals or barrier semaphores. Data moves between devices by JAX's collectives and lax.ppermute only.
A program may use at most 128 MiB of HBM per device.

```python
import math
import jax
import jax.numpy as jnp
from jax import lax

TILE = 128
TC = 4
NT = 64
N = 8192
LIVE = 32
N_ROW = 4
N_COL = 16


def draw_tile_mask(key, part):
    key_score = jax.random.fold_in(key, 11)
    key_count = jax.random.fold_in(key, 12)
    block_rows = NT // N_ROW
    cells = block_rows * TC
    rows_idx = lax.broadcasted_iota(jnp.int32, (NT, NT), 0)
    cols_idx = lax.broadcasted_iota(jnp.int32, (NT, NT), 1)
    local = rows_idx % block_rows * TC + cols_idx % TC
    scores = jax.random.randint(key_score, (NT, NT), 0, 2 ** 20) * cells + local
    scores = jnp.where(rows_idx == cols_idx, scores + 2 ** 28, scores)
    blocks = scores.reshape(N_ROW, block_rows, N_COL, TC).transpose(0, 2, 1, 3).reshape(N_ROW, N_COL, cells)
    order = jnp.argsort(-blocks, axis=-1, stable=True)
    rank = jnp.argsort(order, axis=-1, stable=True).astype(jnp.int32)
    counts = jax.random.randint(key_count, (N_ROW, N_COL), TC, LIVE + 1)
    counts = counts.at[0, 0].set(LIVE)
    active = (rank < counts[:, :, None]).astype(jnp.int32)
    active = active.reshape(N_ROW, N_COL, block_rows, TC).transpose(0, 2, 1, 3).reshape(NT, NT)
    return active.astype(jnp.int32)


def block_levels(own_key, shape, pieces, least, largest):
    gain = 1.0
    for dim, blocks in pieces:
        steps = jax.random.uniform(jax.random.fold_in(jax.random.fold_in(own_key, 6), dim), (blocks,), jnp.float32, least / len(pieces), largest / len(pieces))
        gain = gain * jnp.repeat(jnp.exp(steps), shape[dim] // blocks).reshape((-1,) + (1,) * (len(shape) - 1 - dim))
    return gain


def setup_inputs(seed: int = 0) -> dict:
    keys = jax.random.split(jax.random.key(seed), 3)
    return {
        "values": jnp.clip(jnp.exp(math.log(1.0) - 4.61031033 * jax.random.uniform(keys[0], (N, N), jnp.float32) ** block_levels(keys[0], (N, N), ((0, 4), (1, 16)), -0.2, 0.2)), 0.0099487305, 1.0).astype(jnp.bfloat16),
        "tile_mask": draw_tile_mask(jax.random.fold_in(keys[2], 71), 0),
    }


def reference(values, tile_mask):
    grid = values.reshape(NT, TILE, NT, TILE) * tile_mask.astype(jnp.bfloat16)[:, None, :, None]
    masked = grid.reshape(N, N)
    mass = jnp.sum(masked, axis=0, dtype=jnp.float32)
    stochastic = (masked.astype(jnp.float32) / mass[None, :]).astype(jnp.bfloat16)
    expanded = jnp.dot(stochastic, stochastic, preferred_element_type=jnp.float32)
    inflated = expanded * expanded
    weight = jnp.sum(inflated, axis=0)
    return (N * 1.0) * inflated / weight[None, :]
```

```python
import functools

import jax
import jax.numpy as jnp
from jax import lax
from jax.experimental import pallas as pl
from jax.experimental.pallas import tpu as pltpu
from jax.sharding import PartitionSpec as P

T = 128
HEAD = 16
SCALE = 16.0
VMEM = pl.BlockSpec(memory_space=pltpu.VMEM)
SMEM = pl.BlockSpec(memory_space=pltpu.SMEM)


def pack_kernel(mask_ref, values_ref, packed_ref, sums_ref, table_ref, acc_ref):
    tiles_r, tiles_c = mask_ref.shape
    slots = table_ref.shape[0]
    dead = tiles_r * tiles_c
    acc_ref[...] = jnp.zeros_like(acc_ref)
    for s in range(slots):
        table_ref[s] = dead
    lane = lax.broadcasted_iota(jnp.int32, (HEAD, T), 1)

    def body(i, carry):
        n, head = carry
        for c in range(tiles_c):
            live = mask_ref[i, c] != 0

            @pl.when(live)
            def _():
                tile = values_ref[pl.ds(pl.multiple_of(i * T, T), T), c * T:(c + 1) * T]
                packed_ref[pl.ds(pl.multiple_of(HEAD + n * T, HEAD), T), :] = tile
                acc_ref[c] += jnp.sum(tile.astype(jnp.float32).reshape(T // 8, 8, T), axis=0)
                table_ref[n] = i * tiles_c + c

            head = jnp.where((lane == n) & live, i * tiles_c + c, head)
            n = n + live.astype(jnp.int32)
        return n, head

    start = (jnp.int32(0), jnp.full((HEAD, T), dead, jnp.int32))
    n, head = lax.fori_loop(0, tiles_r, body, start)
    packed_ref[:HEAD, :] = head.astype(jnp.float32).astype(jnp.bfloat16)

    def clear(s, _):
        packed_ref[pl.ds(pl.multiple_of(HEAD + s * T, HEAD), T), :] = jnp.zeros((T, T), jnp.bfloat16)
        return 0

    lax.fori_loop(n, slots, clear, 0)
    for c in range(tiles_c):
        sums_ref[c:c + 1, :] = jnp.sum(acc_ref[c], axis=0, keepdims=True)


def pack(mask, values, slots):
    tiles_r, tiles_c = mask.shape
    return pl.pallas_call(
        pack_kernel,
        out_shape=(
            jax.ShapeDtypeStruct((HEAD + slots * T, T), jnp.bfloat16),
            jax.ShapeDtypeStruct((tiles_c, T), jnp.float32),
            jax.ShapeDtypeStruct((slots,), jnp.int32),
        ),
        in_specs=[SMEM, VMEM],
        out_specs=(VMEM, VMEM, SMEM),
        scratch_shapes=[pltpu.VMEM((tiles_c, 8, T), jnp.float32)],
        cost_estimate=pl.CostEstimate(flops=2**20, bytes_accessed=3 * 2**20, transcendentals=0),
        name="pack",
    )(mask, values)


def slice_kernel(halves, info_ref, table_ref, packed_ref, mass_ref, part_ref):
    layer, section = info_ref[0], info_ref[1]
    tiles_c = mass_ref.shape[0]
    slots = table_ref.shape[0]
    n_layer = slots // (halves * ((part_ref.shape[0] // halves - HEAD) // T))
    per = slots // n_layer // halves
    size = HEAD + per * T
    lane = lax.broadcasted_iota(jnp.int32, (HEAD, T), 1)
    for h in range(halves):
        head = jnp.full((HEAD, T), 256, jnp.int32)
        for j in range(per):
            s = layer * (halves * per) + h * per + j
            t = table_ref[s]
            r, c = lax.div(t, tiles_c), lax.rem(t, tiles_c)
            head = jnp.where(lane == j, r * (4 * tiles_c) + section * tiles_c + c, head)
            tile = packed_ref[pl.ds(pl.multiple_of(HEAD + s * T, HEAD), T), :].astype(jnp.float32)
            out = tile / mass_ref[pl.ds(c, 1), :]
            part_ref[h * size + HEAD + j * T:h * size + HEAD + (j + 1) * T, :] = out.astype(jnp.bfloat16)
        head = jnp.minimum(head, 256)
        part_ref[h * size:h * size + HEAD, :] = head.astype(jnp.float32).astype(jnp.bfloat16)


def left_slice(info, table, packed, mass, per, halves):
    return pl.pallas_call(
        functools.partial(slice_kernel, halves),
        out_shape=jax.ShapeDtypeStruct((halves * (HEAD + per * T), T), jnp.bfloat16),
        in_specs=[SMEM, SMEM, VMEM, VMEM],
        out_specs=VMEM,
        cost_estimate=pl.CostEstimate(flops=2**20, bytes_accessed=2**20, transcendentals=0),
        name="left_slice",
    )(info, table, packed, mass)


def product_kernel(n_parts, sizes, per, *refs):
    info_ref, lidx_ref, ridx_ref = refs[:3]
    part_refs = refs[3:3 + n_parts]
    right_ref = refs[3 + n_parts]
    own_ref, c1_ref, c2_ref, c3_ref = refs[4 + n_parts:8 + n_parts]
    left, right = refs[8 + n_parts:]
    layer = info_ref[0]
    rows, depth = left.shape
    rows = rows - T
    width = right.shape[1]
    kt, ct = depth // T, width // T

    def zero_left(i, _):
        left[pl.ds(pl.multiple_of(i * T, T), T), :] = jnp.zeros((T, depth), jnp.bfloat16)
        return 0

    lax.fori_loop(0, rows // T, zero_left, 0)

    def zero_right(i, _):
        right[pl.ds(pl.multiple_of(i * T, T), T), :] = jnp.zeros((T, width), jnp.bfloat16)
        return 0

    lax.fori_loop(0, depth // T, zero_right, 0)
    q = 0
    for ref, halves in zip(part_refs, sizes, strict=True):
        size = HEAD + per * T
        for h in range(halves):
            for j in range(per):
                t = lidx_ref[q]
                q += 1
                i, k = lax.div(t, kt), lax.rem(t, kt)
                left[pl.ds(pl.multiple_of(i * T, T), T), pl.ds(pl.multiple_of(k * T, T), T)] = (
                    ref[h * size + HEAD + j * T:h * size + HEAD + (j + 1) * T, :]
                )
    slots = ridx_ref.shape[0]

    def put_right(s, _):
        t = ridx_ref[s]
        i, c = lax.div(t, ct), lax.rem(lax.rem(t, ct) + ct - layer, ct)
        right[pl.ds(pl.multiple_of(i * T, T), T), pl.ds(pl.multiple_of(c * T, T), T)] = (
            right_ref[pl.ds(pl.multiple_of(HEAD + s * T, HEAD), T), :]
        )
        return 0

    lax.fori_loop(0, slots, put_right, 0)
    block = 256

    def multiply(m, _):
        at = pl.ds(pl.multiple_of(m * block, block), block)
        out = SCALE * jnp.dot(left[at, :], right[:depth, :], preferred_element_type=jnp.float32)
        own_ref[at, :] = out[:, :T]
        for g, ref in enumerate((c1_ref, c2_ref, c3_ref)):
            ref[at, :] = out[:, (g + 1) * T:(g + 2) * T].astype(ref.dtype)
        return 0

    lax.fori_loop(0, rows // block, multiply, 0)


def product(info, lidx, ridx, parts, sizes, per, right, rows, depth, width):
    n_parts = len(parts)
    send = jax.ShapeDtypeStruct((rows, T), jnp.float32)
    return pl.pallas_call(
        functools.partial(product_kernel, n_parts, sizes, per),
        out_shape=(jax.ShapeDtypeStruct((rows, T), jnp.float32), send, send, send),
        in_specs=[SMEM, SMEM, SMEM] + [VMEM] * (n_parts + 1),
        out_specs=(VMEM,) * 4,
        scratch_shapes=[
            pltpu.VMEM((rows + T, depth), jnp.bfloat16),
            pltpu.VMEM((depth + T, width), jnp.bfloat16),
        ],
        cost_estimate=pl.CostEstimate(flops=2 * rows * depth * width, bytes_accessed=8 * 2**20, transcendentals=0),
        compiler_params=pltpu.CompilerParams(vmem_limit_bytes=48 * 2**20),
        name="product",
    )(info, lidx, ridx, *parts, right)


def coords(sizes):
    n_row, n_col, n_layer = sizes
    for r in range(n_row):
        for c in range(n_col):
            for y in range(n_layer):
                yield r, c, y


def flat(r, c, y, sizes):
    return (r * sizes[1] + c) * sizes[2] + y


def shards(sizes, values, tile_mask):
    n_row, n_col, n_layer = sizes
    axes = ("row", "col", "layer")
    height, width = values.shape
    slots = tile_mask.size // 2
    halves = 2
    per = slots // n_layer // halves
    n_z = n_col // 2
    z_lo = n_z // n_layer

    col, layer = lax.axis_index("col"), lax.axis_index("layer")
    z, x_hi = col // 2, col % 2
    section = (z % z_lo) * 2 + x_hi
    info = jnp.stack([layer, section]).astype(jnp.int32)

    packed, sums, table = pack(tile_mask, values, slots)

    n_x = n_row // 2 * 2
    perm = []
    for r, c, y in coords(sizes):
        x_lo, core, zz, hi = r // 2, r % 2, c // 2, c % 2
        x = hi * 2 + x_lo
        y_to = r
        x_to = (x + 2 - (y - y_to)) % n_x
        to = ((x_to % 2) * 2 + hi, zz * 2 + x_to // 2, y_to)
        perm.append((flat(r, c, y, sizes), flat(*to, sizes)))
    right = lax.ppermute(packed, axes, perm)

    mass = lax.psum(sums, "row")
    part = left_slice(info, table, packed, mass, per, halves)

    perm = []
    for r, c, y in coords(sizes):
        x_lo, core, zz, hi = r // 2, r % 2, c // 2, c % 2
        to = (x_lo * 2 + hi, (y * z_lo + zz % z_lo) * 2 + core, zz // z_lo)
        perm.append((flat(r, c, y, sizes), flat(*to, sizes)))
    part = lax.ppermute(part, axes, perm)

    def ring(step):
        return [(c, (c // 2 + step) % n_z * 2 + c % 2) for c in range(n_col)]

    half = HEAD + per * T
    mine = [part]
    up = down = part
    for step in range(1, n_z // 2 + 1):
        if step == n_z // 2:
            up, down = up[:half], down[half:]
        up = lax.ppermute(up, "col", ring(1))
        down = lax.ppermute(down, "col", ring(-1))
        mine += [up, down]
    swap = [(r, r ^ 1) for r in range(n_row)]
    parts = mine + [lax.ppermute(p, "row", swap) for p in mine]
    counts = [p.shape[0] // half for p in parts]
    lidx = jnp.concatenate(
        [p.reshape(n, half, T)[:, 0, :per].reshape(-1) for p, n in zip(parts, counts, strict=True)]
    ).astype(jnp.int32)
    ridx = right[0, :slots].astype(jnp.int32)
    depth = height * n_row // n_layer
    own, c1, c2, c3 = product(info, lidx, ridx, parts, counts, per, right, height, depth, width)

    up = [(y, (y + 1) % n_layer) for y in range(n_layer)]
    down = [(y, (y - 1) % n_layer) for y in range(n_layer)]
    mid = height // 2
    f16, f32 = jnp.float16, jnp.float32
    far_a = lax.ppermute(c2[:mid].astype(f16), "layer", up)
    far_b = lax.ppermute(c2[mid:].astype(f16), "layer", down)
    up_b = lax.ppermute(c1[mid:].astype(f16), "layer", up)
    down_a = lax.ppermute(c3[:mid].astype(f16), "layer", down)
    up_a = lax.ppermute((c1[:mid] + far_a.astype(f32)).astype(f16), "layer", up)
    down_b = lax.ppermute((c3[mid:] + far_b.astype(f32)).astype(f16), "layer", down)
    total = jnp.concatenate([
        own[:mid] + (up_a.astype(f32) + down_a.astype(f32)),
        own[mid:] + (up_b.astype(f32) + down_b.astype(f32)),
    ]).astype(f16)

    perm = []
    for r in range(n_row):
        for c in range(n_col):
            to = (r // 2 * 2 + c % 2, c // 2 * 2 + r % 2)
            perm.append((r * n_col + c, to[0] * n_col + to[1]))
    expanded = lax.ppermute(total, ("row", "col"), perm).astype(f32)
    inflated = expanded * expanded
    weight = lax.psum(jnp.sum(inflated, axis=0), "row")
    order = height * n_row
    return order * 1.0 * inflated / weight[None, :]


def solution(mesh):
    sizes = tuple(mesh.shape[a] for a in ("row", "col", "layer"))
    return jax.shard_map(
        functools.partial(shards, sizes),
        mesh=mesh,
        in_specs=(P("row", "col"), P("row", "col")),
        out_specs=P("row", ("col", "layer")),
        check_vma=False,
    )
```

```python
import functools

import jax
import jax.numpy as jnp
from jax import lax
from jax.experimental import pallas as pl
from jax.experimental.pallas import tpu as pltpu
from jax.sharding import PartitionSpec as P

T = 128
HEAD = 16
SCALE = 16.0
VMEM = pl.BlockSpec(memory_space=pltpu.VMEM)
SMEM = pl.BlockSpec(memory_space=pltpu.SMEM)


def pack_kernel(halves, per, depth_tiles, info_ref, mask_ref, values_ref, part_ref, sums_ref, acc_ref):
    layer, section = info_ref[0], info_ref[1]
    tiles_r, tiles_c = mask_ref.shape
    dead = tiles_r * depth_tiles
    size = HEAD + per * T
    acc_ref[...] = jnp.zeros_like(acc_ref)
    row = lax.broadcasted_iota(jnp.int32, (HEAD, T), 0)

    def clear(s, _):
        part_ref[pl.ds(pl.multiple_of(s * HEAD, HEAD), HEAD), :] = jnp.zeros((HEAD, T), jnp.bfloat16)
        return 0

    lax.fori_loop(0, halves * size // HEAD, clear, 0)

    def body(i, carry):
        n, heads = carry
        for c in range(tiles_c):
            live = mask_ref[i, c] != 0
            mine = live & (n >= 0) & (n < halves * per)
            at = i * depth_tiles + section * tiles_c + c

            @pl.when(live)
            def _():
                tile = values_ref[pl.ds(pl.multiple_of(i * T, T), T), c * T:(c + 1) * T]
                acc_ref[c] += jnp.sum(tile.astype(jnp.float32).reshape(T // 8, 8, T), axis=0)

            @pl.when(mine)
            def _():
                tile = values_ref[pl.ds(pl.multiple_of(i * T, T), T), c * T:(c + 1) * T]
                start = lax.div(n, per) * size + HEAD + lax.rem(n, per) * T
                part_ref[pl.ds(pl.multiple_of(start, HEAD), T), :] = tile

            heads = tuple(
                jnp.where((row == n - h * per) & (n < (h + 1) * per) & live, at, head)
                for h, head in enumerate(heads)
            )
            n = n + live.astype(jnp.int32)
        return n, heads

    start = (-layer * (halves * per), (jnp.full((HEAD, T), dead, jnp.int32),) * halves)
    _, heads = lax.fori_loop(0, tiles_r, body, start)
    for h, head in enumerate(heads):
        part_ref[h * size:h * size + HEAD, :] = head.astype(jnp.float32).astype(jnp.bfloat16)
    for c in range(tiles_c):
        sums_ref[c:c + 1, :] = jnp.sum(acc_ref[c], axis=0, keepdims=True)


def pack(info, mask, values, per, halves, depth_tiles):
    tiles_c = mask.shape[1]
    return pl.pallas_call(
        functools.partial(pack_kernel, halves, per, depth_tiles),
        out_shape=(
            jax.ShapeDtypeStruct((halves * (HEAD + per * T), T), jnp.bfloat16),
            jax.ShapeDtypeStruct((tiles_c, T), jnp.float32),
        ),
        in_specs=[SMEM, SMEM, VMEM],
        out_specs=(VMEM, VMEM),
        scratch_shapes=[pltpu.VMEM((tiles_c, 8, T), jnp.float32)],
        cost_estimate=pl.CostEstimate(flops=2**20, bytes_accessed=2 * 2**20, transcendentals=0),
        name="pack",
    )(info, mask, values)


def scale_kernel(halves, per, raw_ref, mass_ref, part_ref):
    size = HEAD + per * T
    tiles_c = mass_ref.shape[0]
    for h in range(halves):
        head = raw_ref[h * size:h * size + HEAD, :]
        part_ref[h * size:h * size + HEAD, :] = head
        which = lax.rem(head.astype(jnp.float32).astype(jnp.int32), tiles_c)
        for j in range(per):
            mine = which[j:j + 1, :]
            mass = mass_ref[0:1, :]
            for c in range(1, tiles_c):
                mass = jnp.where(mine == c, mass_ref[c:c + 1, :], mass)
            at = slice(h * size + HEAD + j * T, h * size + HEAD + (j + 1) * T)
            part_ref[at, :] = (raw_ref[at, :].astype(jnp.float32) / mass).astype(jnp.bfloat16)


def scale(raw, mass, per, halves):
    return pl.pallas_call(
        functools.partial(scale_kernel, halves, per),
        out_shape=jax.ShapeDtypeStruct(raw.shape, raw.dtype),
        in_specs=[VMEM, VMEM],
        out_specs=VMEM,
        cost_estimate=pl.CostEstimate(flops=2**20, bytes_accessed=2**20, transcendentals=0),
        name="scale",
    )(raw, mass)


def product_kernel(n_parts, counts, per, *refs):
    info_ref = refs[0]
    part_refs = refs[1:1 + n_parts]
    right_refs = refs[1 + n_parts:3 + n_parts]
    out_ref = refs[3 + n_parts]
    left, spots, table, sem = refs[4 + n_parts:]
    layer = info_ref[0]
    rows, depth = left.shape
    rows = rows - T
    n_layer = out_ref.shape[0]
    kt = depth // T
    size = HEAD + per * T

    lane = lax.broadcasted_iota(jnp.int32, (8, T), 1)
    found = jnp.zeros((8, T), jnp.int32)
    q = 0
    for ref, count in zip(part_refs, counts, strict=True):
        for h in range(count):
            head = ref[h * size:h * size + HEAD, :].astype(jnp.float32).astype(jnp.int32)
            found = jnp.where(lane == q, head[:8, :], found)
            q += 1
    spots[...] = found

    def zero_left(i, _):
        left[pl.ds(pl.multiple_of(i * 64, 64), 64), :] = jnp.zeros((64, depth), jnp.bfloat16)
        return 0

    lax.fori_loop(0, rows // 64, zero_left, 0)
    copy = pltpu.make_async_copy(spots, table, sem)
    copy.start()
    copy.wait()
    q = 0
    for ref, count in zip(part_refs, counts, strict=True):
        for h in range(count):
            for j in range(per):
                t = table[j, q]
                i, k = lax.div(t, kt), lax.rem(t, kt)
                left[pl.ds(pl.multiple_of(i * T, T), T), pl.ds(pl.multiple_of(k * T, T), T)] = (
                    ref[h * size + HEAD + j * T:h * size + HEAD + (j + 1) * T, :]
                )
            q += 1
    block = 256
    mid = depth // 2

    def multiply(m, _):
        at = pl.ds(pl.multiple_of(m * block, block), block)
        out = jnp.dot(left[at, :mid], right_refs[0][...], preferred_element_type=jnp.float32)
        out = out + jnp.dot(left[at, mid:], right_refs[1][...], preferred_element_type=jnp.float32)
        for j in range(n_layer):
            out_ref[lax.rem(j + n_layer - layer, n_layer), at, :] = SCALE * out[:, j * T:(j + 1) * T]
        return 0

    lax.fori_loop(0, rows // block, multiply, 0)


def product(info, parts, counts, per, rights, rows, depth, n_layer):
    n_parts = len(parts)
    width = rights[0].shape[1]
    return pl.pallas_call(
        functools.partial(product_kernel, n_parts, counts, per),
        out_shape=jax.ShapeDtypeStruct((n_layer, rows, width // n_layer), jnp.float32),
        in_specs=[SMEM] + [VMEM] * (n_parts + 2),
        out_specs=VMEM,
        scratch_shapes=[
            pltpu.VMEM((rows + T, depth), jnp.bfloat16),
            pltpu.VMEM((8, T), jnp.int32),
            pltpu.SMEM((8, T), jnp.int32),
            pltpu.SemaphoreType.DMA,
        ],
        cost_estimate=pl.CostEstimate(flops=2 * rows * depth * width, bytes_accessed=8 * 2**20, transcendentals=0),
        compiler_params=pltpu.CompilerParams(vmem_limit_bytes=48 * 2**20),
        name="product",
    )(info, *parts, *rights)


def coords(sizes):
    n_row, n_col, n_layer = sizes
    for r in range(n_row):
        for c in range(n_col):
            for y in range(n_layer):
                yield r, c, y


def flat(r, c, y, sizes):
    return (r * sizes[1] + c) * sizes[2] + y


def shards(sizes, values, tile_mask):
    n_row, n_col, n_layer = sizes
    axes = ("row", "col", "layer")
    height, width = values.shape
    tiles_r, tiles_c = tile_mask.shape
    slots = tile_mask.size // 2
    halves = 2
    per = slots // n_layer // halves
    n_z = n_col // 2
    depth = height * n_row // n_layer
    f16, f32 = jnp.float16, jnp.float32

    row, col, layer = lax.axis_index("row"), lax.axis_index("col"), lax.axis_index("layer")
    x_lo, z, x_hi = row // 2, col // 2, col % 2
    section = ((z // n_layer) ^ (z % 2)) * 2 + x_hi
    info = jnp.stack([layer, section]).astype(jnp.int32)

    raw, sums = pack(info, tile_mask, values, per, halves, depth // T)

    spread = []
    for r, c, y in coords(sizes):
        zz, hi = c // 2, c % 2
        y_to = zz % n_layer
        move = {0: 2 - 4 * hi, 1: 1, 2: 0, 3: -1}[(y - y_to) % n_layer]
        to = (r // 2 * 2 + hi, (zz + move) % n_z * 2 + r % 2, y_to)
        spread.append((flat(r, c, y, sizes), flat(*to, sizes)))
    raw = lax.ppermute(raw, axes, spread)
    mass = lax.ppermute(lax.psum(sums, "row"), axes, spread)
    part = scale(raw, mass, per, halves)

    masked = (
        values.reshape(tiles_r, T, tiles_c, T)
        * tile_mask.astype(jnp.bfloat16)[:, None, :, None]
    ).reshape(2, height // 2, width)
    rights = [lax.dynamic_index_in_dim(masked, m ^ x_lo, 0, keepdims=False) for m in range(2)]
    *rights, raw = lax.optimization_barrier((*rights, raw))
    n_x = n_row // 2 * 2
    for m in range(2):
        perm = []
        for r, c, y in coords(sizes):
            lo, core, zz, hi = r // 2, r % 2, c // 2, c % 2
            y_to = core * 2 + (m ^ lo)
            x_to = (hi * 2 + lo + 2 - (y - y_to)) % n_x
            to = (x_to % 2 * 2 + hi, zz * 2 + x_to // 2, y_to)
            perm.append((flat(r, c, y, sizes), flat(*to, sizes)))
        rights[m] = lax.ppermute(rights[m], axes, perm)

    def ring(step):
        return [(c, (c // 2 + step) % n_z * 2 + c % 2) for c in range(n_col)]

    half = HEAD + per * T
    mine = [part]
    up = down = part
    for step in range(1, n_z // 2 + 1):
        if step == n_z // 2:
            up, down = up[:half], down[half:]
        up = lax.ppermute(up, "col", ring(1))
        down = lax.ppermute(down, "col", ring(-1))
        mine += [up, down]
    swap = [(r, r ^ 1) for r in range(n_row)]
    parts = mine + [lax.ppermute(p, "row", swap) for p in mine]
    counts = [p.shape[0] // half for p in parts]
    out = product(info, parts, counts, per, rights, height, depth, n_layer)

    up = [(y, (y + 1) % n_layer) for y in range(n_layer)]
    down = [(y, (y - 1) % n_layer) for y in range(n_layer)]
    mid = height // 2
    send = lax.optimization_barrier(out[1:].astype(f16))
    far_a = lax.ppermute(send[1, :mid], "layer", up)
    far_b = lax.ppermute(send[1, mid:], "layer", down)
    up_b = lax.ppermute(send[0, mid:], "layer", up)
    down_a = lax.ppermute(send[2, :mid], "layer", down)
    up_a = lax.ppermute((out[1, :mid] + far_a.astype(f32)).astype(f16), "layer", up)
    down_b = lax.ppermute((out[3, mid:] + far_b.astype(f32)).astype(f16), "layer", down)
    total = jnp.concatenate([
        out[0, :mid] + (up_a.astype(f32) + down_a.astype(f32)),
        out[0, mid:] + (up_b.astype(f32) + down_b.astype(f32)),
    ]).astype(f16)

    perm = []
    for r in range(n_row):
        for c in range(n_col):
            to = (r // 2 * 2 + c % 2, c // 2 * 2 + r % 2)
            perm.append((r * n_col + c, to[0] * n_col + to[1]))
    expanded = lax.ppermute(total, ("row", "col"), perm).astype(f32)
    inflated = expanded * expanded
    weight = lax.psum(jnp.sum(inflated, axis=0), "row")
    order = height * n_row
    return order * 1.0 * inflated / weight[None, :]


def solution(mesh):
    sizes = tuple(mesh.shape[a] for a in ("row", "col", "layer"))
    return jax.shard_map(
        functools.partial(shards, sizes),
        mesh=mesh,
        in_specs=(P("row", "col"), P("row", "col")),
        out_specs=P("row", ("col", "layer")),
        check_vma=False,
    )
```

```python
import functools

import jax
import jax.numpy as jnp
from jax import lax
from jax.experimental import pallas as pl
from jax.experimental.pallas import tpu as pltpu
from jax.sharding import PartitionSpec as P


T = 128
HEAD = 16
SCALE = 16.0
VMEM = pl.BlockSpec(memory_space=pltpu.VMEM)
ANY = pl.BlockSpec(memory_space=pl.ANY)


def share_kernel(halves, per, depth_tiles, mask_hbm, values_hbm, part_ref, mask_ref, table_ref, sem):
    tiles_r, tiles_c = mask_ref.shape
    layer, col = lax.axis_index("layer"), lax.axis_index("col")
    z = lax.div(col, 2)
    section = ((lax.div(z, 4) ^ (z & 1)) * 2) + (col & 1)
    dead = tiles_r * tiles_c
    count = halves * per
    size = HEAD + per * T
    copy = pltpu.make_async_copy(mask_hbm, mask_ref, sem)
    copy.start()
    copy.wait()
    for s in range(count):
        table_ref[s] = dead
    n = -layer * count
    for i in range(tiles_r):
        for c in range(tiles_c):
            live = mask_ref[i, c] != 0
            spot = jnp.where(live & (n >= 0) & (n < count), n, count)
            table_ref[spot] = i * tiles_c + c
            n = n + live.astype(jnp.int32)
    starts = [(s // per) * size + HEAD + (s % per) * T for s in range(count)]

    def fetch(s):
        t = table_ref[s]
        i, c = lax.div(t, tiles_c), lax.rem(t, tiles_c)
        return pltpu.make_async_copy(
            values_hbm.at[pl.ds(pl.multiple_of(i * T, T), T), pl.ds(pl.multiple_of(c * T, T), T)],
            part_ref.at[starts[s]:starts[s] + T, :],
            sem,
        )

    for s in range(count):
        @pl.when(table_ref[s] < dead)
        def _():
            fetch(s).start()

        @pl.when(table_ref[s] >= dead)
        def _():
            part_ref[starts[s]:starts[s] + T, :] = jnp.zeros((T, T), jnp.bfloat16)

    row = lax.broadcasted_iota(jnp.int32, (HEAD, T), 0)
    for h in range(halves):
        head = jnp.full((HEAD, T), tiles_r * depth_tiles, jnp.int32)
        for j in range(per):
            t = table_ref[h * per + j]
            at = lax.div(t, tiles_c) * depth_tiles + section * tiles_c + lax.rem(t, tiles_c)
            head = jnp.where((row == j) & (t < dead), at, head)
        part_ref[h * size:h * size + HEAD, :] = head.astype(jnp.float32).astype(jnp.bfloat16)
    for s in range(count):
        @pl.when(table_ref[s] < dead)
        def _():
            fetch(s).wait()


def share(mask, values, per, halves, depth_tiles):
    return pl.pallas_call(
        functools.partial(share_kernel, halves, per, depth_tiles),
        out_shape=jax.ShapeDtypeStruct((halves * (HEAD + per * T), T), jnp.bfloat16),
        in_specs=[ANY, ANY],
        out_specs=VMEM,
        scratch_shapes=[
            pltpu.SMEM(mask.shape, jnp.int32),
            pltpu.SMEM((halves * per + 1,), jnp.int32),
            pltpu.SemaphoreType.DMA,
        ],
        cost_estimate=pl.CostEstimate(flops=2**20, bytes_accessed=2 * 2**20, transcendentals=0),
        name="share",
    )(mask, values)


def mask_kernel(mask_hbm, values_ref, out_ref, sums_ref, mask_ref, sem):
    tiles_r, tiles_c = mask_ref.shape
    copy = pltpu.make_async_copy(mask_hbm, mask_ref, sem)
    copy.start()
    copy.wait()
    x_lo = lax.div(lax.axis_index("row"), 2)
    sums = [jnp.zeros((8, T), jnp.float32)] * tiles_c
    for i in range(tiles_r):
        half = (i // (tiles_r // 2)) ^ x_lo
        at = i % (tiles_r // 2) * T
        for c in range(tiles_c):
            tile = values_ref[i * T:(i + 1) * T, c * T:(c + 1) * T]
            tile = jnp.where(mask_ref[i, c] != 0, tile, jnp.zeros_like(tile))
            out_ref[half, at:at + T, c * T:(c + 1) * T] = tile
            sums[c] = sums[c] + jnp.sum(tile.astype(jnp.float32).reshape(T // 8, 8, T), axis=0)
    for c in range(tiles_c):
        sums_ref[c:c + 1, :] = jnp.sum(sums[c], axis=0, keepdims=True)


def mask_block(mask, values):
    height, width = values.shape
    return pl.pallas_call(
        mask_kernel,
        out_shape=(
            jax.ShapeDtypeStruct((2, height // 2, width), jnp.bfloat16),
            jax.ShapeDtypeStruct((mask.shape[1], T), jnp.float32),
        ),
        in_specs=[ANY, VMEM],
        out_specs=(VMEM, VMEM),
        scratch_shapes=[pltpu.SMEM(mask.shape, jnp.int32), pltpu.SemaphoreType.DMA],
        cost_estimate=pl.CostEstimate(flops=2**20, bytes_accessed=4 * 2**20, transcendentals=0),
        name="mask_block",
    )(mask, values)


def scale_kernel(halves, per, raw_ref, *refs):
    mass_refs, part_ref = refs[:-1], refs[-1]
    size = HEAD + per * T
    sums = mass_refs[0][...]
    for ref in mass_refs[1:]:
        sums = sums + ref[...]
    tiles_c = sums.shape[0]
    for h in range(halves):
        head = raw_ref[h * size:h * size + HEAD, :]
        part_ref[h * size:h * size + HEAD, :] = head
        which = lax.rem(head.astype(jnp.float32).astype(jnp.int32), tiles_c)
        for j in range(per):
            mine = which[j:j + 1, :]
            mass = sums[0:1, :]
            for c in range(1, tiles_c):
                mass = jnp.where(mine == c, sums[c:c + 1, :], mass)
            at = slice(h * size + HEAD + j * T, h * size + HEAD + (j + 1) * T)
            part_ref[at, :] = (raw_ref[at, :].astype(jnp.float32) / mass).astype(jnp.bfloat16)


def scale(raw, masses, per, halves):
    return pl.pallas_call(
        functools.partial(scale_kernel, halves, per),
        out_shape=jax.ShapeDtypeStruct(raw.shape, raw.dtype),
        in_specs=[VMEM] * (1 + len(masses)),
        out_specs=VMEM,
        cost_estimate=pl.CostEstimate(flops=2**20, bytes_accessed=2**20, transcendentals=0),
        name="scale",
    )(raw, *masses)


def product_kernel(n_parts, counts, per, *refs):
    part_refs = refs[:n_parts]
    right_refs = refs[n_parts:2 + n_parts]
    out_ref = refs[2 + n_parts]
    left, spots, table, sem = refs[3 + n_parts:]
    layer = lax.axis_index("layer")
    rows, depth = left.shape
    rows = rows - T
    n_layer = out_ref.shape[0]
    kt = depth // T
    size = HEAD + per * T

    lane = lax.broadcasted_iota(jnp.int32, (8, T), 1)
    found = jnp.zeros((8, T), jnp.int32)
    q = 0
    for ref, count in zip(part_refs, counts, strict=True):
        for h in range(count):
            head = ref[h * size:h * size + HEAD, :].astype(jnp.float32).astype(jnp.int32)
            found = jnp.where(lane == q, head[:8, :], found)
            q += 1
    spots[...] = found

    def zero_left(i, _):
        left[pl.ds(pl.multiple_of(i * 64, 64), 64), :] = jnp.zeros((64, depth), jnp.bfloat16)
        return 0

    lax.fori_loop(0, rows // 64, zero_left, 0)
    copy = pltpu.make_async_copy(spots, table, sem)
    copy.start()
    copy.wait()
    q = 0
    for ref, count in zip(part_refs, counts, strict=True):
        for h in range(count):
            for j in range(per):
                t = table[j, q]
                i, k = lax.div(t, kt), lax.rem(t, kt)
                left[pl.ds(pl.multiple_of(i * T, T), T), pl.ds(pl.multiple_of(k * T, T), T)] = (
                    ref[h * size + HEAD + j * T:h * size + HEAD + (j + 1) * T, :]
                )
            q += 1
    block = 256
    mid = depth // 2

    def multiply(m, _):
        at = pl.ds(pl.multiple_of(m * block, block), block)
        out = jnp.dot(left[at, :mid], right_refs[0][...], preferred_element_type=jnp.float32)
        out = out + jnp.dot(left[at, mid:], right_refs[1][...], preferred_element_type=jnp.float32)
        for j in range(n_layer):
            out_ref[lax.rem(j + n_layer - layer, n_layer), at, :] = SCALE * out[:, j * T:(j + 1) * T]
        return 0

    lax.fori_loop(0, rows // block, multiply, 0)


def product(parts, counts, per, rights, rows, depth, n_layer):
    n_parts = len(parts)
    width = rights[0].shape[1]
    return pl.pallas_call(
        functools.partial(product_kernel, n_parts, counts, per),
        out_shape=jax.ShapeDtypeStruct((n_layer, rows, width // n_layer), jnp.float32),
        in_specs=[VMEM] * (n_parts + 2),
        out_specs=VMEM,
        scratch_shapes=[
            pltpu.VMEM((rows + T, depth), jnp.bfloat16),
            pltpu.VMEM((8, T), jnp.int32),
            pltpu.SMEM((8, T), jnp.int32),
            pltpu.SemaphoreType.DMA,
        ],
        cost_estimate=pl.CostEstimate(flops=2 * rows * depth * width, bytes_accessed=8 * 2**20, transcendentals=0),
        compiler_params=pltpu.CompilerParams(vmem_limit_bytes=48 * 2**20),
        name="product",
    )(*parts, *rights)


def coords(sizes):
    n_row, n_col, n_layer = sizes
    for r in range(n_row):
        for c in range(n_col):
            for y in range(n_layer):
                yield r, c, y


def flat(r, c, y, sizes):
    return (r * sizes[1] + c) * sizes[2] + y


def named(array, axes, perm):
    return lax.ppermute(array, axes, perm)


def shards(sizes, values, tile_mask):
    n_row, n_col, n_layer = sizes
    axes = ("row", "col", "layer")
    height, _ = values.shape
    slots = tile_mask.size // 2
    halves = 2
    per = slots // n_layer // halves
    half = HEAD + per * T
    n_z = n_col // 2
    depth = height * n_row // n_layer
    f16, f32 = jnp.float16, jnp.float32

    raw = share(tile_mask, values, per, halves, depth // T)

    spread = {}
    for r, c, y in coords(sizes):
        zz, hi = c // 2, c % 2
        y_to = zz % n_layer
        move = {0: 2 - 4 * hi, 1: 1, 2: 0, 3: -1}[(y - y_to) % n_layer]
        spread[r, c, y] = flat(r // 2 * 2 + hi, (zz + move) % n_z * 2 + r % 2, y_to, sizes)
    raw = named(raw, axes, [(flat(*at, sizes), to) for at, to in spread.items()])
    masked, sums = mask_block(tile_mask, values)
    masses = [
        named(sums, axes, [(flat(r, c, y, sizes), spread[r ^ k, c, y]) for r, c, y in coords(sizes)])
        for k in range(n_row)
    ]
    part = scale(raw, masses, per, halves)

    def ring(step):
        return [(c, (c // 2 + step) % n_z * 2 + c % 2) for c in range(n_col)]

    chains = {(k, d): part[k * half:(k + 1) * half] for k in range(halves) for d in (1, -1)}
    mine = [chains[k, 1] for k in range(halves)]
    for step in range(1, n_z // 2 + 1):
        for (k, d) in list(chains):
            if step == n_z // 2 and (k == 0) != (d == 1):
                continue
            chains[k, d] = named(chains[k, d], "col", ring(d))
            mine.append(chains[k, d])
    swap = [(r, r ^ 1) for r in range(n_row)]
    parts = mine + [named(p, "row", swap) for p in mine]

    n_x = n_row // 2 * 2
    rights = []
    for m in range(2):
        perm = []
        for r, c, y in coords(sizes):
            lo, core, zz, hi = r // 2, r % 2, c // 2, c % 2
            y_to = core * 2 + (m ^ lo)
            x_to = (hi * 2 + lo + 2 - (y - y_to)) % n_x
            lo_to, hi_to = x_to % 2, x_to // 2
            to = (lo_to * 2 + (hi ^ hi_to ^ lo_to ^ 1), zz * 2 + hi_to, y_to)
            perm.append((flat(r, c, y, sizes), flat(*to, sizes)))
        rights.append(named(masked[m], axes, perm))
    out = product(parts, [1] * len(parts), per, rights, height, depth, n_layer)

    up = [(y, (y + 1) % n_layer) for y in range(n_layer)]
    down = [(y, (y - 1) % n_layer) for y in range(n_layer)]
    mid = height // 2
    send = lax.optimization_barrier(out[1:].astype(f16))
    far_a = named(send[1, :mid], "layer", up)
    far_b = named(send[1, mid:], "layer", down)
    up_b = named(send[0, mid:], "layer", up)
    down_a = named(send[2, :mid], "layer", down)
    up_a = named((out[1, :mid] + far_a.astype(f32)).astype(f16), "layer", up)
    down_b = named((out[3, mid:] + far_b.astype(f32)).astype(f16), "layer", down)
    total = jnp.concatenate([
        out[0, :mid] + (up_a.astype(f32) + down_a.astype(f32)),
        out[0, mid:] + (up_b.astype(f32) + down_b.astype(f32)),
    ]).astype(f16)

    owner = {}
    for r in range(n_row):
        for c in range(n_col):
            lo, core, hi = r // 2, r % 2, c % 2
            owner[r, c] = (lo * 2 + hi, c // 2 * 2 + (core ^ hi ^ lo ^ 1))
    expanded = named(
        total, ("row", "col"), [(r * n_col + c, o[0] * n_col + o[1]) for (r, c), o in owner.items()])
    summand = total.astype(f32)
    summand = jnp.sum(summand * summand, axis=0)
    weight = 0.0
    for k in range(n_row):
        perm = [(r * n_col + c, (o[0] ^ k) * n_col + o[1]) for (r, c), o in owner.items()]
        weight = weight + named(summand, ("row", "col"), perm)
    expanded = expanded.astype(f32)
    inflated = expanded * expanded
    order = height * n_row
    return order * 1.0 * inflated / weight[None, :]


def solution(mesh):
    sizes = tuple(mesh.shape[a] for a in ("row", "col", "layer"))

    def body(values, tile_mask):
        return shards(sizes, values, tile_mask)

    return jax.shard_map(
        body,
        mesh=mesh,
        in_specs=(P("row", "col"), P("row", "col")),
        out_specs=P("row", ("col", "layer")),
        check_vma=False,
    )
```

```python
import functools

import jax
import jax.numpy as jnp
from jax import lax
from jax.experimental import pallas as pl
from jax.experimental.pallas import tpu as pltpu
from jax.sharding import PartitionSpec as P


T = 128
HEAD = 16
SCALE = 16.0
GRANT = 16 * 2**20
VMEM = pl.BlockSpec(memory_space=pltpu.VMEM)
HBM = pl.BlockSpec(memory_space=pltpu.HBM)
ANY = pl.BlockSpec(memory_space=pl.ANY)


def share_kernel(halves, per, depth_tiles, mask_hbm, values_hbm, part_ref, mask_ref, table_ref, sem):
    tiles_c, tiles_r = mask_ref.shape
    layer, col = lax.axis_index("layer"), lax.axis_index("col")
    z = lax.div(col, 2)
    section = ((lax.div(z, 4) ^ (z & 1)) * 2) + (col & 1)
    dead = tiles_r * tiles_c
    count = halves * per
    size = HEAD + per * T
    copy = pltpu.make_async_copy(mask_hbm, mask_ref, sem)
    copy.start()
    copy.wait()
    for s in range(count):
        table_ref[s] = dead
    n = -layer * count
    for i in range(tiles_r):
        for c in range(tiles_c):
            live = mask_ref[c, i] != 0
            spot = jnp.where(live & (n >= 0) & (n < count), n, count)
            table_ref[spot] = i * tiles_c + c
            n = n + live.astype(jnp.int32)
    starts = [(s // per) * size + HEAD + (s % per) * T for s in range(count)]

    def fetch(s):
        t = table_ref[s]
        i, c = lax.div(t, tiles_c), lax.rem(t, tiles_c)
        return pltpu.make_async_copy(
            values_hbm.at[pl.ds(pl.multiple_of(i * T, T), T), pl.ds(pl.multiple_of(c * T, T), T)],
            part_ref.at[starts[s]:starts[s] + T, :],
            sem,
        )

    for s in range(count):
        @pl.when(table_ref[s] < dead)
        def _():
            fetch(s).start()

        @pl.when(table_ref[s] >= dead)
        def _():
            part_ref[starts[s]:starts[s] + T, :] = jnp.zeros((T, T), jnp.bfloat16)

    row = lax.broadcasted_iota(jnp.int32, (HEAD, T), 0)
    for h in range(halves):
        head = jnp.full((HEAD, T), tiles_r * depth_tiles, jnp.int32)
        for j in range(per):
            t = table_ref[h * per + j]
            at = lax.div(t, tiles_c) * depth_tiles + section * tiles_c + lax.rem(t, tiles_c)
            head = jnp.where((row == j) & (t < dead), at, head)
        part_ref[h * size:h * size + HEAD, :] = head.astype(jnp.float32).astype(jnp.bfloat16)
    for s in range(count):
        @pl.when(table_ref[s] < dead)
        def _():
            fetch(s).wait()


def share(mask, values, per, halves, depth_tiles):
    return pl.pallas_call(
        functools.partial(share_kernel, halves, per, depth_tiles),
        out_shape=pltpu.VMEM((halves * (HEAD + per * T), T), jnp.bfloat16),
        in_specs=[HBM, HBM],
        out_specs=VMEM,
        scratch_shapes=[
            pltpu.SMEM(mask.shape, jnp.int32),
            pltpu.SMEM((halves * per + 1,), jnp.int32),
            pltpu.SemaphoreType.DMA,
        ],
        cost_estimate=pl.CostEstimate(flops=2**20, bytes_accessed=2 * 2**20, transcendentals=0),
        compiler_params=pltpu.CompilerParams(vmem_limit_bytes=GRANT),
        name="share",
    )(mask, values)


def load(mask_hbm, mask_ref, sem):
    copy = pltpu.make_async_copy(mask_hbm, mask_ref, sem)
    copy.start()
    copy.wait()


def sums_kernel(mask_hbm, values_ref, sums_ref, mask_ref, sem):
    tiles_c, tiles_r = mask_ref.shape
    load(mask_hbm, mask_ref, sem)
    for c in range(tiles_c):
        total = jnp.zeros((8, T), jnp.float32)
        for i in range(tiles_r):
            tile = values_ref[i * T:(i + 1) * T, c * T:(c + 1) * T].astype(jnp.float32)
            part = jnp.sum(tile.reshape(T // 8, 8, T), axis=0)
            total = total + jnp.where(mask_ref[c, i] != 0, part, 0.0)
        sums_ref[c:c + 1, :] = jnp.sum(total, axis=0, keepdims=True)


def column_sums(mask, values):
    return pl.pallas_call(
        sums_kernel,
        out_shape=pltpu.VMEM((mask.shape[0], T), jnp.float32),
        in_specs=[ANY, VMEM],
        out_specs=VMEM,
        scratch_shapes=[pltpu.SMEM(mask.shape, jnp.int32), pltpu.SemaphoreType.DMA],
        cost_estimate=pl.CostEstimate(flops=2**20, bytes_accessed=2 * 2**20, transcendentals=0),
        compiler_params=pltpu.CompilerParams(vmem_limit_bytes=GRANT),
        name="column_sums",
    )(mask, values)


def halves_kernel(mask_hbm, values_ref, *refs):
    out_refs, (mask_ref, sem) = refs[:2], refs[2:]
    tiles_c, tiles_r = mask_ref.shape
    load(mask_hbm, mask_ref, sem)
    x_lo = lax.div(lax.axis_index("row"), 2)
    for m, ref in enumerate(out_refs):
        first = (m ^ x_lo) * (tiles_r // 2)
        for i in range(tiles_r // 2):
            at = pl.ds(pl.multiple_of((first + i) * T, T), T)
            for c in range(tiles_c):
                tile = values_ref[at, c * T:(c + 1) * T]
                ref[i * T:(i + 1) * T, c * T:(c + 1) * T] = jnp.where(
                    mask_ref[c, first + i] != 0, tile, jnp.zeros_like(tile))


def masked_halves(mask, values):
    height, width = values.shape
    return pl.pallas_call(
        halves_kernel,
        out_shape=(pltpu.VMEM((height // 2, width), jnp.bfloat16),) * 2,
        in_specs=[ANY, VMEM],
        out_specs=(VMEM, VMEM),
        scratch_shapes=[pltpu.SMEM(mask.shape, jnp.int32), pltpu.SemaphoreType.DMA],
        cost_estimate=pl.CostEstimate(flops=2**20, bytes_accessed=4 * 2**20, transcendentals=0),
        compiler_params=pltpu.CompilerParams(vmem_limit_bytes=GRANT),
        name="masked_halves",
    )(mask, values)


def scale_kernel(halves, per, raw_ref, mass_ref, part_ref):
    size = HEAD + per * T
    sums = mass_ref[...] / SCALE
    tiles_c = sums.shape[0]
    for h in range(halves):
        head = raw_ref[h * size:h * size + HEAD, :]
        part_ref[h * size:h * size + HEAD, :] = head
        which = lax.rem(head.astype(jnp.float32).astype(jnp.int32), tiles_c)
        for j in range(per):
            mine = which[j:j + 1, :]
            mass = sums[0:1, :]
            for c in range(1, tiles_c):
                mass = jnp.where(mine == c, sums[c:c + 1, :], mass)
            at = slice(h * size + HEAD + j * T, h * size + HEAD + (j + 1) * T)
            part_ref[at, :] = (raw_ref[at, :].astype(jnp.float32) / mass).astype(jnp.bfloat16)


def scale(raw, mass, per, halves):
    return pl.pallas_call(
        functools.partial(scale_kernel, halves, per),
        out_shape=pltpu.VMEM(raw.shape, raw.dtype),
        in_specs=[VMEM, VMEM],
        out_specs=VMEM,
        cost_estimate=pl.CostEstimate(flops=2**20, bytes_accessed=2**20, transcendentals=0),
        compiler_params=pltpu.CompilerParams(vmem_limit_bytes=GRANT),
        name="scale",
    )(raw, mass)


def product_kernel(n_parts, counts, per, again, *refs):
    part_refs = refs[:n_parts]
    right_refs = refs[n_parts:2 + n_parts]
    out_ref = refs[2 + n_parts + again]
    spots, table, sem = refs[3 + n_parts + again:]
    layer = lax.axis_index("layer")
    n_layer, rows, _ = out_ref.shape
    depth = right_refs[0].shape[0]
    kt = 2 * depth // T
    dead = rows // T * kt
    size = HEAD + per * T

    lane = lax.broadcasted_iota(jnp.int32, (8, T), 1)
    found = jnp.zeros((8, T), jnp.int32)
    q = 0
    for ref, count in zip(part_refs, counts, strict=True):
        for h in range(count):
            head = ref[h * size:h * size + HEAD, :].astype(jnp.float32).astype(jnp.int32)
            found = jnp.where(lane == q, head[:8, :], found)
            q += 1
    spots[...] = found
    if not again:
        def zero(i, _):
            out_ref[:, pl.ds(pl.multiple_of(i * T, T), T), :] = jnp.zeros((n_layer, T, T), jnp.float32)
            return 0

        lax.fori_loop(0, rows // T, zero, 0)
    copy = pltpu.make_async_copy(spots, table, sem)
    copy.start()
    copy.wait()
    q = 0
    for ref, count in zip(part_refs, counts, strict=True):
        def add(s, _, ref=ref, q=q):
            h, j = lax.div(s, per), lax.rem(s, per)
            t = table[j, q + h]
            tile = pl.ds(pl.multiple_of(h * size + HEAD + j * T, HEAD), T)
            k = lax.rem(t, kt)
            at = pl.ds(pl.multiple_of(lax.div(t, kt) * T, T), T)
            rows_of = pl.ds(pl.multiple_of(lax.rem(k, kt // 2) * T, T), T)
            for m, right_ref in enumerate(right_refs):
                @pl.when((t < dead) & (lax.div(k, kt // 2) == m))
                def _():
                    out = jnp.dot(ref[tile, :], right_ref[rows_of, :], preferred_element_type=jnp.float32)
                    for g in range(n_layer):
                        chunk = lax.rem(g + n_layer - layer, n_layer)
                        out_ref[chunk, at, :] += out[:, g * T:(g + 1) * T]
            return 0

        lax.fori_loop(0, count * per, add, 0)
        q += count


def product(parts, counts, per, rights, rows, n_layer, total=None):
    n_parts = len(parts)
    width = rights[0].shape[1]
    again = total is not None
    tiles = sum(counts) * per
    return pl.pallas_call(
        functools.partial(product_kernel, n_parts, counts, per, again),
        out_shape=pltpu.VMEM((n_layer, rows, width // n_layer), jnp.float32),
        in_specs=[VMEM] * (n_parts + 2 + again),
        out_specs=VMEM,
        scratch_shapes=[
            pltpu.VMEM((8, T), jnp.int32),
            pltpu.SMEM((8, T), jnp.int32),
            pltpu.SemaphoreType.DMA,
        ],
        input_output_aliases={n_parts + 2: 0} if again else {},
        cost_estimate=pl.CostEstimate(flops=2 * tiles * T * T * width, bytes_accessed=2**20, transcendentals=0),
        compiler_params=pltpu.CompilerParams(vmem_limit_bytes=GRANT),
        name="add_product" if again else "product",
    )(*parts, *rights, *((total,) if again else ()))


def coords(sizes):
    n_row, n_col, n_layer = sizes
    for r in range(n_row):
        for c in range(n_col):
            for y in range(n_layer):
                yield r, c, y


def flat(r, c, y, sizes):
    return (r * sizes[1] + c) * sizes[2] + y


def shards(sizes, values, tile_mask):
    n_row, n_col, n_layer = sizes
    axes = ("row", "col", "layer")
    height, _ = values.shape
    slots = tile_mask.size // 2
    halves = 2
    per = slots // n_layer // halves
    half = HEAD + per * T
    n_z = n_col // 2
    depth = height * n_row // n_layer
    f16, f32 = jnp.float16, jnp.float32

    mask = tile_mask.T
    raw = share(mask, values, per, halves, depth // T)

    spread = {}
    for r, c, y in coords(sizes):
        zz, hi = c // 2, c % 2
        y_to = zz % n_layer
        move = {0: 2 - 4 * hi, 1: 1, 2: 0, 3: -1}[(y - y_to) % n_layer]
        spread[r, c, y] = flat(r // 2 * 2 + hi, (zz + move) % n_z * 2 + r % 2, y_to, sizes)
    table = [(flat(*at, sizes), to) for at, to in spread.items()]
    raw = lax.ppermute(raw, axes, table)
    mass = lax.ppermute(lax.psum(column_sums(mask, values), "row"), axes, table)
    rights = list(masked_halves(mask, values))
    part = scale(raw, mass, per, halves)

    def ring(step):
        return [(c, (c // 2 + step) % n_z * 2 + c % 2) for c in range(n_col)]

    swap = [(r, r ^ 1) for r in range(n_row)]
    last = n_z // 2
    mine = [part]
    up = down = part
    for step in range(1, last + 1):
        if step == last:
            up, down = up[:half], down[half:]
        up = lax.ppermute(up, "col", ring(1))
        down = lax.ppermute(down, "col", ring(-1))
        mine += [up, down]
    parts = [(p, lax.ppermute(p, "row", swap)) for p in mine]

    n_x = n_row // 2 * 2
    for m in range(2):
        perm = []
        for r, c, y in coords(sizes):
            lo, core, zz, hi = r // 2, r % 2, c // 2, c % 2
            y_to = core * 2 + (m ^ lo)
            x_to = (hi * 2 + lo + 2 - (y - y_to)) % n_x
            lo_to, hi_to = x_to % 2, x_to // 2
            to = (lo_to * 2 + (hi ^ hi_to ^ lo_to ^ 1), zz * 2 + hi_to, y_to)
            perm.append((flat(r, c, y, sizes), flat(*to, sizes)))
        rights[m] = lax.ppermute(rights[m], axes, perm)
    early = [p for pair in parts[:2 * last - 3] for p in pair]
    late = [p for pair in parts[2 * last - 3:] for p in pair]
    out = product(early, [p.shape[0] // half for p in early], per, rights, height, n_layer)
    out = product(late, [p.shape[0] // half for p in late], per, rights, height, n_layer, out)

    up = [(y, (y + 1) % n_layer) for y in range(n_layer)]
    down = [(y, (y - 1) % n_layer) for y in range(n_layer)]
    mid = height // 2
    send = lax.optimization_barrier(out[1:].astype(f16))
    far_a = lax.ppermute(send[1, :mid], "layer", up)
    far_b = lax.ppermute(send[1, mid:], "layer", down)
    up_b = lax.ppermute(send[0, mid:], "layer", up)
    down_a = lax.ppermute(send[2, :mid], "layer", down)
    up_a = (out[1, :mid] + far_a.astype(f32)).astype(f16)
    down_b = (out[3, mid:] + far_b.astype(f32)).astype(f16)
    up_a, down_b = lax.optimization_barrier((up_a, down_b))
    up_a = lax.ppermute(up_a, "layer", up)
    down_b = lax.ppermute(down_b, "layer", down)
    total = jnp.concatenate([
        out[0, :mid] + (up_a.astype(f32) + down_a.astype(f32)),
        out[0, mid:] + (up_b.astype(f32) + down_b.astype(f32)),
    ]).astype(f16)

    owner = {}
    for r in range(n_row):
        for c in range(n_col):
            lo, core, hi = r // 2, r % 2, c % 2
            owner[r, c] = (lo * 2 + hi, c // 2 * 2 + (core ^ hi ^ lo ^ 1))
    expanded = lax.ppermute(
        total, ("row", "col"), [(r * n_col + c, o[0] * n_col + o[1]) for (r, c), o in owner.items()])
    summand = total.astype(f32)
    summand = jnp.sum(summand * summand, axis=0)
    weights = []
    for k in range(1, n_row):
        perm = [(r * n_col + c, (o[0] ^ k) * n_col + o[1]) for (r, c), o in owner.items()]
        weights.append(lax.ppermute(summand, ("row", "col"), perm))
    expanded = expanded.astype(f32)
    inflated = expanded * expanded
    weight = jnp.sum(inflated, axis=0) + (weights[0] + (weights[1] + weights[2]))
    order = height * n_row
    return order * 1.0 * inflated / weight[None, :]


def solution(mesh):
    sizes = tuple(mesh.shape[a] for a in ("row", "col", "layer"))

    def body(values, tile_mask):
        return shards(sizes, values, tile_mask)

    return jax.shard_map(
        body,
        mesh=mesh,
        in_specs=(P("row", "col"), P("row", "col")),
        out_specs=P("row", ("col", "layer")),
        check_vma=False,
    )
```

```python
import functools

import jax
import jax.numpy as jnp
from jax import lax
from jax.experimental import pallas as pl
from jax.experimental.pallas import tpu as pltpu
from jax.sharding import PartitionSpec as P


T = 128
HEAD = 16
SCALE = 16.0
GRANT = 16 * 2**20
VMEM = pl.BlockSpec(memory_space=pltpu.VMEM)
HBM = pl.BlockSpec(memory_space=pltpu.HBM)
ANY = pl.BlockSpec(memory_space=pl.ANY)


def share_kernel(halves, per, depth_tiles, mask_hbm, values_hbm, part_ref, mask_ref, table_ref, sem):
    tiles_c, tiles_r = mask_ref.shape
    layer, col = lax.axis_index("layer"), lax.axis_index("col")
    z = lax.div(col, 2)
    section = ((lax.div(z, 4) ^ (z & 1)) * 2) + (col & 1)
    dead = tiles_r * tiles_c
    count = halves * per
    size = HEAD + per * T
    copy = pltpu.make_async_copy(mask_hbm, mask_ref, sem)
    copy.start()
    copy.wait()
    for s in range(count):
        table_ref[s] = dead
    n = -layer * count
    for i in range(tiles_r):
        for c in range(tiles_c):
            live = mask_ref[c, i] != 0
            spot = jnp.where(live & (n >= 0) & (n < count), n, count)
            table_ref[spot] = i * tiles_c + c
            n = n + live.astype(jnp.int32)
    starts = [(s // per) * size + HEAD + (s % per) * T for s in range(count)]

    def fetch(s):
        t = table_ref[s]
        i, c = lax.div(t, tiles_c), lax.rem(t, tiles_c)
        return pltpu.make_async_copy(
            values_hbm.at[pl.ds(pl.multiple_of(i * T, T), T), pl.ds(pl.multiple_of(c * T, T), T)],
            part_ref.at[starts[s]:starts[s] + T, :],
            sem,
        )

    for s in range(count):
        @pl.when(table_ref[s] < dead)
        def _():
            fetch(s).start()

        @pl.when(table_ref[s] >= dead)
        def _():
            part_ref[starts[s]:starts[s] + T, :] = jnp.zeros((T, T), jnp.bfloat16)

    row = lax.broadcasted_iota(jnp.int32, (HEAD, T), 0)
    for h in range(halves):
        head = jnp.full((HEAD, T), tiles_r * depth_tiles, jnp.int32)
        for j in range(per):
            t = table_ref[h * per + j]
            at = lax.div(t, tiles_c) * depth_tiles + section * tiles_c + lax.rem(t, tiles_c)
            head = jnp.where((row == j) & (t < dead), at, head)
        part_ref[h * size:h * size + HEAD, :] = head.astype(jnp.float32).astype(jnp.bfloat16)
    for s in range(count):
        @pl.when(table_ref[s] < dead)
        def _():
            fetch(s).wait()


def share(mask, values, per, halves, depth_tiles):
    return pl.pallas_call(
        functools.partial(share_kernel, halves, per, depth_tiles),
        out_shape=pltpu.VMEM((halves * (HEAD + per * T), T), jnp.bfloat16),
        in_specs=[HBM, HBM],
        out_specs=VMEM,
        scratch_shapes=[
            pltpu.SMEM(mask.shape, jnp.int32),
            pltpu.SMEM((halves * per + 1,), jnp.int32),
            pltpu.SemaphoreType.DMA,
        ],
        cost_estimate=pl.CostEstimate(flops=2**20, bytes_accessed=2 * 2**20, transcendentals=0),
        compiler_params=pltpu.CompilerParams(vmem_limit_bytes=GRANT),
        name="share",
    )(mask, values)


def load(mask_hbm, mask_ref, sem):
    copy = pltpu.make_async_copy(mask_hbm, mask_ref, sem)
    copy.start()
    copy.wait()


def sums_kernel(mask_hbm, values_ref, sums_ref, mask_ref, sem):
    tiles_c, tiles_r = mask_ref.shape
    load(mask_hbm, mask_ref, sem)
    for c in range(tiles_c):
        total = jnp.zeros((8, T), jnp.float32)
        for i in range(tiles_r):
            tile = values_ref[i * T:(i + 1) * T, c * T:(c + 1) * T].astype(jnp.float32)
            part = jnp.sum(tile.reshape(T // 8, 8, T), axis=0)
            total = total + jnp.where(mask_ref[c, i] != 0, part, 0.0)
        sums_ref[c:c + 1, :] = jnp.sum(total, axis=0, keepdims=True)


def column_sums(mask, values):
    return pl.pallas_call(
        sums_kernel,
        out_shape=pltpu.VMEM((mask.shape[0], T), jnp.float32),
        in_specs=[ANY, VMEM],
        out_specs=VMEM,
        scratch_shapes=[pltpu.SMEM(mask.shape, jnp.int32), pltpu.SemaphoreType.DMA],
        cost_estimate=pl.CostEstimate(flops=2**20, bytes_accessed=2 * 2**20, transcendentals=0),
        compiler_params=pltpu.CompilerParams(vmem_limit_bytes=GRANT),
        name="column_sums",
    )(mask, values)


def halves_kernel(mask_hbm, values_ref, *refs):
    out_refs, (mask_ref, sem) = refs[:2], refs[2:]
    tiles_c, tiles_r = mask_ref.shape
    load(mask_hbm, mask_ref, sem)
    x_lo = lax.div(lax.axis_index("row"), 2)
    for m, ref in enumerate(out_refs):
        first = (m ^ x_lo) * (tiles_r // 2)
        for i in range(tiles_r // 2):
            at = pl.ds(pl.multiple_of((first + i) * T, T), T)
            for c in range(tiles_c):
                tile = values_ref[at, c * T:(c + 1) * T]
                ref[i * T:(i + 1) * T, c * T:(c + 1) * T] = jnp.where(
                    mask_ref[c, first + i] != 0, tile, jnp.zeros_like(tile))


def masked_halves(mask, values):
    height, width = values.shape
    return pl.pallas_call(
        halves_kernel,
        out_shape=(pltpu.VMEM((height // 2, width), jnp.bfloat16),) * 2,
        in_specs=[ANY, VMEM],
        out_specs=(VMEM, VMEM),
        scratch_shapes=[pltpu.SMEM(mask.shape, jnp.int32), pltpu.SemaphoreType.DMA],
        cost_estimate=pl.CostEstimate(flops=2**20, bytes_accessed=4 * 2**20, transcendentals=0),
        compiler_params=pltpu.CompilerParams(vmem_limit_bytes=GRANT),
        name="masked_halves",
    )(mask, values)


def scale_kernel(halves, per, raw_ref, mass_ref, part_ref):
    size = HEAD + per * T
    sums = mass_ref[...] / SCALE
    tiles_c = sums.shape[0]
    for h in range(halves):
        head = raw_ref[h * size:h * size + HEAD, :]
        part_ref[h * size:h * size + HEAD, :] = head
        which = lax.rem(head.astype(jnp.float32).astype(jnp.int32), tiles_c)
        for j in range(per):
            mine = which[j:j + 1, :]
            mass = sums[0:1, :]
            for c in range(1, tiles_c):
                mass = jnp.where(mine == c, sums[c:c + 1, :], mass)
            at = slice(h * size + HEAD + j * T, h * size + HEAD + (j + 1) * T)
            part_ref[at, :] = (raw_ref[at, :].astype(jnp.float32) / mass).astype(jnp.bfloat16)


def scale(raw, mass, per, halves):
    return pl.pallas_call(
        functools.partial(scale_kernel, halves, per),
        out_shape=pltpu.VMEM(raw.shape, raw.dtype),
        in_specs=[VMEM, VMEM],
        out_specs=VMEM,
        cost_estimate=pl.CostEstimate(flops=2**20, bytes_accessed=2**20, transcendentals=0),
        compiler_params=pltpu.CompilerParams(vmem_limit_bytes=GRANT),
        name="scale",
    )(raw, mass)


def product_kernel(n_parts, counts, per, again, *refs):
    part_refs = refs[:n_parts]
    right_ref = refs[n_parts]
    out_ref = refs[1 + n_parts + again]
    spots, table, sem = refs[2 + n_parts + again:]
    layer = lax.axis_index("layer")
    n_layer, rows, _ = out_ref.shape
    kt = right_ref.shape[0] // T
    chunks = [lax.rem(g + n_layer - layer, n_layer) for g in range(n_layer)]
    size = HEAD + per * T

    lane = lax.broadcasted_iota(jnp.int32, (8, T), 1)
    found = jnp.zeros((8, T), jnp.int32)
    q = 0
    for ref, count in zip(part_refs, counts, strict=True):
        for h in range(count):
            head = ref[h * size:h * size + HEAD, :].astype(jnp.float32).astype(jnp.int32)
            found = jnp.where(lane == q, head[:8, :], found)
            q += 1
    spots[...] = found
    if not again:
        def zero(i, _):
            out_ref[:, pl.ds(pl.multiple_of(i * T, T), T), :] = jnp.zeros((n_layer, T, T), jnp.float32)
            return 0

        lax.fori_loop(0, rows // T, zero, 0)
    copy = pltpu.make_async_copy(spots, table, sem)
    copy.start()
    copy.wait()
    q = 0
    for ref, count in zip(part_refs, counts, strict=True):
        for h in range(count):
            for j in range(per):
                t = table[j, q]
                at = pl.ds(pl.multiple_of(lax.div(t, kt) * T, T), T)
                rows_of = pl.ds(pl.multiple_of(lax.rem(t, kt) * T, T), T)
                tile = ref[h * size + HEAD + j * T:h * size + HEAD + (j + 1) * T, :]
                out = jnp.dot(tile, right_ref[rows_of, :], preferred_element_type=jnp.float32)
                for g, chunk in enumerate(chunks):
                    out_ref[chunk, at, :] += out[:, g * T:(g + 1) * T]
            q += 1


def product(parts, counts, per, right, rows, n_layer, total=None):
    n_parts = len(parts)
    width = right.shape[1]
    again = total is not None
    tiles = sum(counts) * per
    return pl.pallas_call(
        functools.partial(product_kernel, n_parts, counts, per, again),
        out_shape=pltpu.VMEM((n_layer, rows + T, width // n_layer), jnp.float32),
        in_specs=[VMEM] * (n_parts + 1 + again),
        out_specs=VMEM,
        scratch_shapes=[
            pltpu.VMEM((8, T), jnp.int32),
            pltpu.SMEM((8, T), jnp.int32),
            pltpu.SemaphoreType.DMA,
        ],
        input_output_aliases={n_parts + 1: 0} if again else {},
        cost_estimate=pl.CostEstimate(flops=2 * tiles * T * T * width, bytes_accessed=2**20, transcendentals=0),
        compiler_params=pltpu.CompilerParams(vmem_limit_bytes=GRANT),
        name="add_product" if again else "product",
    )(*parts, right, *((total,) if again else ()))


def coords(sizes):
    n_row, n_col, n_layer = sizes
    for r in range(n_row):
        for c in range(n_col):
            for y in range(n_layer):
                yield r, c, y


def flat(r, c, y, sizes):
    return (r * sizes[1] + c) * sizes[2] + y


def shards(sizes, values, tile_mask):
    n_row, n_col, n_layer = sizes
    axes = ("row", "col", "layer")
    height, _ = values.shape
    slots = tile_mask.size // 2
    halves = 2
    per = slots // n_layer // halves
    half = HEAD + per * T
    n_z = n_col // 2
    depth = height * n_row // n_layer
    f16, f32 = jnp.float16, jnp.float32

    mask = tile_mask.T
    hbm = functools.partial(pltpu.with_memory_space_constraint, memory_space=pltpu.HBM)
    raw = share(hbm(mask), hbm(values), per, halves, depth // T)

    spread = {}
    for r, c, y in coords(sizes):
        zz, hi = c // 2, c % 2
        y_to = zz % n_layer
        move = {0: 2 - 4 * hi, 1: 1, 2: 0, 3: -1}[(y - y_to) % n_layer]
        spread[r, c, y] = flat(r // 2 * 2 + hi, (zz + move) % n_z * 2 + r % 2, y_to, sizes)
    table = [(flat(*at, sizes), to) for at, to in spread.items()]
    raw = lax.ppermute(raw, axes, table)
    mass = lax.ppermute(lax.psum(column_sums(mask, values), "row"), axes, table)
    rights = list(masked_halves(mask, values))
    part = scale(raw, mass, per, halves)

    def ring(step):
        return [(c, (c // 2 + step) % n_z * 2 + c % 2) for c in range(n_col)]

    swap = [(r, r ^ 1) for r in range(n_row)]
    last = n_z // 2
    mine = [part]
    up = down = part
    for step in range(1, last + 1):
        if step == last:
            up, down = up[:half], down[half:]
        up = lax.ppermute(up, "col", ring(1))
        down = lax.ppermute(down, "col", ring(-1))
        mine += [up, down]
    parts = [(p, lax.ppermute(p, "row", swap)) for p in mine]

    n_x = n_row // 2 * 2
    for m in range(2):
        perm = []
        for r, c, y in coords(sizes):
            lo, core, zz, hi = r // 2, r % 2, c // 2, c % 2
            y_to = core * 2 + (m ^ lo)
            x_to = (hi * 2 + lo + 2 - (y - y_to)) % n_x
            lo_to, hi_to = x_to % 2, x_to // 2
            to = (lo_to * 2 + (hi ^ hi_to ^ lo_to ^ 1), zz * 2 + hi_to, y_to)
            perm.append((flat(r, c, y, sizes), flat(*to, sizes)))
        rights[m] = lax.ppermute(rights[m], axes, perm)
    right = jnp.concatenate(rights)
    early = [p for pair in parts[:2 * last - 3] for p in pair]
    late = [p for pair in parts[2 * last - 3:] for p in pair]
    out = product(early, [p.shape[0] // half for p in early], per, right, height, n_layer)
    out = product(late, [p.shape[0] // half for p in late], per, right, height, n_layer, out)

    up = [(y, (y + 1) % n_layer) for y in range(n_layer)]
    down = [(y, (y - 1) % n_layer) for y in range(n_layer)]
    mid = height // 2
    send = lax.optimization_barrier(out[1:, :height].astype(f16))
    far_a = lax.ppermute(send[1, :mid], "layer", up)
    far_b = lax.ppermute(send[1, mid:], "layer", down)
    up_b = lax.ppermute(send[0, mid:], "layer", up)
    down_a = lax.ppermute(send[2, :mid], "layer", down)
    up_a = (out[1, :mid] + far_a.astype(f32)).astype(f16)
    down_b = (out[3, mid:height] + far_b.astype(f32)).astype(f16)
    up_a, down_b = lax.optimization_barrier((up_a, down_b))
    up_a = lax.ppermute(up_a, "layer", up)
    down_b = lax.ppermute(down_b, "layer", down)
    total = jnp.concatenate([
        out[0, :mid] + (up_a.astype(f32) + down_a.astype(f32)),
        out[0, mid:height] + (up_b.astype(f32) + down_b.astype(f32)),
    ]).astype(f16)

    owner = {}
    for r in range(n_row):
        for c in range(n_col):
            lo, core, hi = r // 2, r % 2, c % 2
            owner[r, c] = (lo * 2 + hi, c // 2 * 2 + (core ^ hi ^ lo ^ 1))
    expanded = lax.ppermute(
        total, ("row", "col"), [(r * n_col + c, o[0] * n_col + o[1]) for (r, c), o in owner.items()])
    summand = total.astype(f32)
    summand = jnp.sum(summand * summand, axis=0)
    row, x_hi = lax.axis_index("row"), lax.axis_index("col") % 2
    which = (row % 2) ^ x_hi ^ (row // 2) ^ 1
    pair = jnp.where(lax.broadcasted_iota(jnp.int32, (2, T), 0) == which, summand, 0.0)
    pair = lax.psum(pair, "row")
    pair = pair + lax.ppermute(pair, "col", [(c, c ^ 1) for c in range(n_col)])
    weight = jnp.where(x_hi == 0, pair[0], pair[1])
    expanded = expanded.astype(f32)
    inflated = expanded * expanded
    order = height * n_row
    return order * 1.0 * inflated / weight[None, :]


def solution(mesh):
    sizes = tuple(mesh.shape[a] for a in ("row", "col", "layer"))

    def body(values, tile_mask):
        return shards(sizes, values, tile_mask)

    return jax.shard_map(
        body,
        mesh=mesh,
        in_specs=(P("row", "col"), P("row", "col")),
        out_specs=P("row", ("col", "layer")),
        check_vma=False,
    )
```

```python
import functools

import jax
import jax.numpy as jnp
from jax import lax
from jax.experimental import pallas as pl
from jax.experimental.pallas import tpu as pltpu
from jax.sharding import PartitionSpec as P


T = 128
HEAD = 16
SCALE = 16.0
GRANT = 16 * 2**20
VMEM = pl.BlockSpec(memory_space=pltpu.VMEM)
HBM = pl.BlockSpec(memory_space=pltpu.HBM)
ANY = pl.BlockSpec(memory_space=pl.ANY)


def share_kernel(halves, per, depth_tiles, mask_hbm, values_hbm, part_ref, mask_ref, table_ref, sem):
    tiles_c, tiles_r = mask_ref.shape
    layer, row, z = lax.axis_index("layer"), lax.axis_index("row"), lax.div(lax.axis_index("col"), 2)
    section = lax.div(z, 2) ^ row
    dead = tiles_r * tiles_c
    count = halves * per
    size = HEAD + per * T
    copy = pltpu.make_async_copy(mask_hbm, mask_ref, sem)
    copy.start()
    copy.wait()
    for s in range(count):
        table_ref[s] = dead
    n = -layer * count
    for i in range(tiles_r):
        for c in range(tiles_c):
            live = mask_ref[c, i] != 0
            spot = jnp.where(live & (n >= 0) & (n < count), n, count)
            table_ref[spot] = i * tiles_c + c
            n = n + live.astype(jnp.int32)
    starts = [(s // per) * size + HEAD + (s % per) * T for s in range(count)]

    def fetch(s):
        t = table_ref[s]
        i, c = lax.div(t, tiles_c), lax.rem(t, tiles_c)
        return pltpu.make_async_copy(
            values_hbm.at[pl.ds(pl.multiple_of(i * T, T), T), pl.ds(pl.multiple_of(c * T, T), T)],
            part_ref.at[starts[s]:starts[s] + T, :],
            sem,
        )

    for s in range(count):
        @pl.when(table_ref[s] < dead)
        def _():
            fetch(s).start()

        @pl.when(table_ref[s] >= dead)
        def _():
            part_ref[starts[s]:starts[s] + T, :] = jnp.zeros((T, T), jnp.bfloat16)

    row = lax.broadcasted_iota(jnp.int32, (HEAD, T), 0)
    for h in range(halves):
        head = jnp.full((HEAD, T), tiles_r * depth_tiles, jnp.int32)
        for j in range(per):
            t = table_ref[h * per + j]
            at = lax.div(t, tiles_c) * depth_tiles + section * tiles_c + lax.rem(t, tiles_c)
            head = jnp.where((row == j) & (t < dead), at, head)
        part_ref[h * size:h * size + HEAD, :] = head.astype(jnp.float32).astype(jnp.bfloat16)
    for s in range(count):
        @pl.when(table_ref[s] < dead)
        def _():
            fetch(s).wait()


def share(mask, values, per, halves, depth_tiles):
    return pl.pallas_call(
        functools.partial(share_kernel, halves, per, depth_tiles),
        out_shape=pltpu.VMEM((halves * (HEAD + per * T), T), jnp.bfloat16),
        in_specs=[HBM, HBM],
        out_specs=VMEM,
        scratch_shapes=[
            pltpu.SMEM(mask.shape, jnp.int32),
            pltpu.SMEM((halves * per + 1,), jnp.int32),
            pltpu.SemaphoreType.DMA,
        ],
        cost_estimate=pl.CostEstimate(flops=2**20, bytes_accessed=2 * 2**20, transcendentals=0),
        compiler_params=pltpu.CompilerParams(vmem_limit_bytes=GRANT),
        name="share",
    )(mask, values)


def load(mask_hbm, mask_ref, sem):
    copy = pltpu.make_async_copy(mask_hbm, mask_ref, sem)
    copy.start()
    copy.wait()


def sums_kernel(mask_hbm, values_ref, sums_ref, mask_ref, sem):
    tiles_c, tiles_r = mask_ref.shape
    load(mask_hbm, mask_ref, sem)
    for c in range(tiles_c):
        total = jnp.zeros((8, T), jnp.float32)
        for i in range(tiles_r):
            tile = values_ref[i * T:(i + 1) * T, c * T:(c + 1) * T].astype(jnp.float32)
            part = jnp.sum(tile.reshape(T // 8, 8, T), axis=0)
            total = total + jnp.where(mask_ref[c, i] != 0, part, 0.0)
        sums_ref[c:c + 1, :] = jnp.sum(total, axis=0, keepdims=True)


def column_sums(mask, values):
    return pl.pallas_call(
        sums_kernel,
        out_shape=pltpu.VMEM((mask.shape[0], T), jnp.float32),
        in_specs=[ANY, VMEM],
        out_specs=VMEM,
        scratch_shapes=[pltpu.SMEM(mask.shape, jnp.int32), pltpu.SemaphoreType.DMA],
        cost_estimate=pl.CostEstimate(flops=2**20, bytes_accessed=2 * 2**20, transcendentals=0),
        compiler_params=pltpu.CompilerParams(vmem_limit_bytes=GRANT),
        name="column_sums",
    )(mask, values)


def quarter_kernel(mask_hbm, values_ref, out_ref, mask_ref, sem):
    tiles_c, _ = mask_ref.shape
    load(mask_hbm, mask_ref, sem)
    layer = lax.axis_index("layer")
    first = ((layer & 1) * 2 + lax.div(layer, 2)) * tiles_c
    for i in range(out_ref.shape[0] // T):
        at = pl.ds(pl.multiple_of((first + i) * T, T), T)
        for c in range(tiles_c):
            tile = values_ref[at, c * T:(c + 1) * T]
            out_ref[i * T:(i + 1) * T, c * T:(c + 1) * T] = jnp.where(
                mask_ref[c, first + i] != 0, tile, jnp.zeros_like(tile))


def masked_quarter(mask, values, n_layer):
    height, width = values.shape
    return pl.pallas_call(
        quarter_kernel,
        out_shape=pltpu.VMEM((height // n_layer, width), jnp.bfloat16),
        in_specs=[ANY, VMEM],
        out_specs=VMEM,
        scratch_shapes=[pltpu.SMEM(mask.shape, jnp.int32), pltpu.SemaphoreType.DMA],
        cost_estimate=pl.CostEstimate(flops=2**18, bytes_accessed=2**20, transcendentals=0),
        compiler_params=pltpu.CompilerParams(vmem_limit_bytes=GRANT),
        name="masked_quarter",
    )(mask, values)


def scale_kernel(halves, per, raw_ref, mass_ref, part_ref):
    size = HEAD + per * T
    sums = mass_ref[...] / SCALE
    tiles_c = sums.shape[0]
    for h in range(halves):
        head = raw_ref[h * size:h * size + HEAD, :]
        part_ref[h * size:h * size + HEAD, :] = head
        which = lax.rem(head.astype(jnp.float32).astype(jnp.int32), tiles_c)
        for j in range(per):
            mine = which[j:j + 1, :]
            mass = sums[0:1, :]
            for c in range(1, tiles_c):
                mass = jnp.where(mine == c, sums[c:c + 1, :], mass)
            at = slice(h * size + HEAD + j * T, h * size + HEAD + (j + 1) * T)
            part_ref[at, :] = (raw_ref[at, :].astype(jnp.float32) / mass).astype(jnp.bfloat16)


def scale(raw, mass, per, halves):
    return pl.pallas_call(
        functools.partial(scale_kernel, halves, per),
        out_shape=pltpu.VMEM(raw.shape, raw.dtype),
        in_specs=[VMEM, VMEM],
        out_specs=VMEM,
        cost_estimate=pl.CostEstimate(flops=2**20, bytes_accessed=2**20, transcendentals=0),
        compiler_params=pltpu.CompilerParams(vmem_limit_bytes=GRANT),
        name="scale",
    )(raw, mass)


def product_kernel(n_parts, counts, per, again, *refs):
    part_refs = refs[:n_parts]
    right_ref = refs[n_parts]
    out_ref = refs[1 + n_parts + again]
    spots, table, sem = refs[2 + n_parts + again:]
    layer = lax.axis_index("layer")
    n_layer, rows, _ = out_ref.shape
    kt = right_ref.shape[0] // T
    chunks = [lax.rem(g + n_layer - layer, n_layer) for g in range(n_layer)]
    size = HEAD + per * T

    lane = lax.broadcasted_iota(jnp.int32, (8, T), 1)
    found = jnp.zeros((8, T), jnp.int32)
    q = 0
    for ref, count in zip(part_refs, counts, strict=True):
        for h in range(count):
            head = ref[h * size:h * size + HEAD, :].astype(jnp.float32).astype(jnp.int32)
            found = jnp.where(lane == q, head[:8, :], found)
            q += 1
    spots[...] = found
    if not again:
        def zero(i, _):
            out_ref[:, pl.ds(pl.multiple_of(i * T, T), T), :] = jnp.zeros((n_layer, T, T), jnp.float32)
            return 0

        lax.fori_loop(0, rows // T, zero, 0)
    copy = pltpu.make_async_copy(spots, table, sem)
    copy.start()
    copy.wait()
    q = 0
    for ref, count in zip(part_refs, counts, strict=True):
        for h in range(count):
            for j in range(per):
                t = table[j, q]
                at = pl.ds(pl.multiple_of(lax.div(t, kt) * T, T), T)
                rows_of = pl.ds(pl.multiple_of(lax.rem(t, kt) * T, T), T)
                tile = ref[h * size + HEAD + j * T:h * size + HEAD + (j + 1) * T, :]
                out = jnp.dot(tile, right_ref[rows_of, :], preferred_element_type=jnp.float32)
                for g, chunk in enumerate(chunks):
                    out_ref[chunk, at, :] += out[:, g * T:(g + 1) * T]
            q += 1


def product(parts, counts, per, right, rows, n_layer, total=None):
    n_parts = len(parts)
    width = right.shape[1]
    again = total is not None
    tiles = sum(counts) * per
    return pl.pallas_call(
        functools.partial(product_kernel, n_parts, counts, per, again),
        out_shape=pltpu.VMEM((n_layer, rows + T, width // n_layer), jnp.float32),
        in_specs=[VMEM] * (n_parts + 1 + again),
        out_specs=VMEM,
        scratch_shapes=[
            pltpu.VMEM((8, T), jnp.int32),
            pltpu.SMEM((8, T), jnp.int32),
            pltpu.SemaphoreType.DMA,
        ],
        input_output_aliases={n_parts + 1: 0} if again else {},
        cost_estimate=pl.CostEstimate(flops=2 * tiles * T * T * width, bytes_accessed=2**20, transcendentals=0),
        compiler_params=pltpu.CompilerParams(vmem_limit_bytes=GRANT),
        name="add_product" if again else "product",
    )(*parts, right, *((total,) if again else ()))


def coords(sizes):
    n_row, n_col, n_layer = sizes
    for r in range(n_row):
        for c in range(n_col):
            for y in range(n_layer):
                yield r, c, y


def flat(r, c, y, sizes):
    return (r * sizes[1] + c) * sizes[2] + y


def shards(sizes, values, tile_mask):
    n_row, n_col, n_layer = sizes
    axes = ("row", "col", "layer")
    height, _ = values.shape
    slots = tile_mask.size // 2
    halves = 2
    per = slots // n_layer // halves
    half = HEAD + per * T
    n_z = n_col // 2
    depth = height * n_row // n_layer
    f16, f32 = jnp.float16, jnp.float32

    mask = tile_mask.T
    hbm = functools.partial(pltpu.with_memory_space_constraint, memory_space=pltpu.HBM)
    raw = share(hbm(mask), hbm(values), per, halves, depth // T)

    spread = {}
    for r, c, y in coords(sizes):
        zz, hi = c // 2, c % 2
        y_to = hi * 2 + zz % 2
        move, core = {0: (1, 0), 1: (-1, 1), 2: (0, 0), 3: (0, 1)}[(y - y_to) % n_layer]
        spread[r, c, y] = flat(r // 2 * 2 + core, (zz + move) % n_z * 2 + r % 2, y_to, sizes)
    table = [(flat(*at, sizes), to) for at, to in spread.items()]
    raw = lax.ppermute(raw, axes, table)
    mass = lax.ppermute(lax.psum(column_sums(mask, values), "row"), axes, table)
    quarter = masked_quarter(mask, values, n_layer)
    part = scale(raw, mass, per, halves)

    def ring(step):
        return [(c, (c // 2 + step) % n_z * 2 + c % 2) for c in range(n_col)]

    swap = [(r, r ^ 1) for r in range(n_row)]
    last = n_z // 2
    mine = [part]
    up = down = part
    for step in range(1, last + 1):
        if step == last:
            up, down = up[:half], down[half:]
        up = lax.ppermute(up, "col", ring(1))
        down = lax.ppermute(down, "col", ring(-1))
        mine += [up, down]
    parts = [(p, lax.ppermute(p, "row", swap)) for p in mine]

    rights = []
    for m in range(n_row):
        perm = []
        for r, c, y in coords(sizes):
            lo, core, zz, hi = r // 2, r % 2, c // 2, c % 2
            lo_to, hi_to = lo ^ m // 2, core ^ m % 2
            to = (lo_to * 2 + (hi ^ hi_to ^ lo_to ^ 1), zz * 2 + hi_to, y)
            perm.append((flat(r, c, y, sizes), flat(*to, sizes)))
        rights.append(lax.ppermute(quarter, axes, perm))
    right = jnp.concatenate(rights)
    early = [p for pair in parts[:2 * last - 3] for p in pair]
    late = [p for pair in parts[2 * last - 3:] for p in pair]
    out = product(early, [p.shape[0] // half for p in early], per, right, height, n_layer)
    out = product(late, [p.shape[0] // half for p in late], per, right, height, n_layer, out)

    up = [(y, (y + 1) % n_layer) for y in range(n_layer)]
    down = [(y, (y - 1) % n_layer) for y in range(n_layer)]
    mid = height // 2
    send = lax.optimization_barrier(out[1:, :height].astype(f16))
    far_a = lax.ppermute(send[1, :mid], "layer", up)
    far_b = lax.ppermute(send[1, mid:], "layer", down)
    up_b = lax.ppermute(send[0, mid:], "layer", up)
    down_a = lax.ppermute(send[2, :mid], "layer", down)
    up_a = (out[1, :mid] + far_a.astype(f32)).astype(f16)
    down_b = (out[3, mid:height] + far_b.astype(f32)).astype(f16)
    up_a, down_b = lax.optimization_barrier((up_a, down_b))
    up_a = lax.ppermute(up_a, "layer", up)
    down_b = lax.ppermute(down_b, "layer", down)
    total = jnp.concatenate([
        out[0, :mid] + (up_a.astype(f32) + down_a.astype(f32)),
        out[0, mid:height] + (up_b.astype(f32) + down_b.astype(f32)),
    ]).astype(f16)

    owner = {}
    for r in range(n_row):
        for c in range(n_col):
            lo, core, hi = r // 2, r % 2, c % 2
            owner[r, c] = (lo * 2 + hi, c // 2 * 2 + (core ^ hi ^ lo ^ 1))
    expanded = lax.ppermute(
        total, ("row", "col"), [(r * n_col + c, o[0] * n_col + o[1]) for (r, c), o in owner.items()])
    summand = total.astype(f32)
    summand = jnp.sum(summand * summand, axis=0)
    weights = []
    for k in range(1, n_row):
        perm = [(r * n_col + c, (o[0] ^ k) * n_col + o[1]) for (r, c), o in owner.items()]
        weights.append(lax.ppermute(summand, ("row", "col"), perm))
    expanded = expanded.astype(f32)
    inflated = expanded * expanded
    weight = jnp.sum(inflated, axis=0) + (weights[0] + (weights[1] + weights[2]))
    order = height * n_row
    return order * 1.0 * inflated / weight[None, :]


def solution(mesh):
    sizes = tuple(mesh.shape[a] for a in ("row", "col", "layer"))

    def body(values, tile_mask):
        return shards(sizes, values, tile_mask)

    return jax.shard_map(
        body,
        mesh=mesh,
        in_specs=(P("row", "col"), P("row", "col")),
        out_specs=P("row", ("col", "layer")),
        check_vma=False,
    )
```

```python
import functools

import jax
import jax.numpy as jnp
from jax import lax
from jax.experimental import pallas as pl
from jax.experimental.pallas import tpu as pltpu
from jax.sharding import PartitionSpec as P


T = 128
HEAD = 16
SCALE = 16.0
GRANT = 16 * 2**20
VMEM = pl.BlockSpec(memory_space=pltpu.VMEM)
HBM = pl.BlockSpec(memory_space=pltpu.HBM)
ANY = pl.BlockSpec(memory_space=pl.ANY)


def share_kernel(halves, per, depth_tiles, mask_hbm, values_hbm, part_ref, mask_ref, table_ref, sem):
    tiles_c, tiles_r = mask_ref.shape
    layer, row, z = lax.axis_index("layer"), lax.axis_index("row"), lax.div(lax.axis_index("col"), 2)
    section = lax.div(z, 2) ^ row
    dead = tiles_r * tiles_c
    count = halves * per
    size = HEAD + per * T
    copy = pltpu.make_async_copy(mask_hbm, mask_ref, sem)
    copy.start()
    copy.wait()
    for s in range(count):
        table_ref[s] = dead
    n = -layer * count
    for i in range(tiles_r):
        for c in range(tiles_c):
            live = mask_ref[c, i] != 0
            spot = jnp.where(live & (n >= 0) & (n < count), n, count)
            table_ref[spot] = i * tiles_c + c
            n = n + live.astype(jnp.int32)
    starts = [(s // per) * size + HEAD + (s % per) * T for s in range(count)]

    def fetch(s):
        t = table_ref[s]
        i, c = lax.div(t, tiles_c), lax.rem(t, tiles_c)
        return pltpu.make_async_copy(
            values_hbm.at[pl.ds(pl.multiple_of(i * T, T), T), pl.ds(pl.multiple_of(c * T, T), T)],
            part_ref.at[starts[s]:starts[s] + T, :],
            sem,
        )

    for s in range(count):
        @pl.when(table_ref[s] < dead)
        def _():
            fetch(s).start()

        @pl.when(table_ref[s] >= dead)
        def _():
            part_ref[starts[s]:starts[s] + T, :] = jnp.zeros((T, T), jnp.bfloat16)

    row = lax.broadcasted_iota(jnp.int32, (HEAD, T), 0)
    for h in range(halves):
        head = jnp.full((HEAD, T), tiles_r * depth_tiles, jnp.int32)
        for j in range(per):
            t = table_ref[h * per + j]
            at = lax.div(t, tiles_c) * depth_tiles + section * tiles_c + lax.rem(t, tiles_c)
            head = jnp.where((row == j) & (t < dead), at, head)
        part_ref[h * size:h * size + HEAD, :] = head.astype(jnp.float32).astype(jnp.bfloat16)
    for s in range(count):
        @pl.when(table_ref[s] < dead)
        def _():
            fetch(s).wait()


def share(mask, values, per, halves, depth_tiles):
    return pl.pallas_call(
        functools.partial(share_kernel, halves, per, depth_tiles),
        out_shape=pltpu.VMEM((halves * (HEAD + per * T), T), jnp.bfloat16),
        in_specs=[HBM, HBM],
        out_specs=VMEM,
        scratch_shapes=[
            pltpu.SMEM(mask.shape, jnp.int32),
            pltpu.SMEM((halves * per + 1,), jnp.int32),
            pltpu.SemaphoreType.DMA,
        ],
        cost_estimate=pl.CostEstimate(flops=2**20, bytes_accessed=2 * 2**20, transcendentals=0),
        compiler_params=pltpu.CompilerParams(vmem_limit_bytes=GRANT),
        name="share",
    )(mask, values)


def load(mask_hbm, mask_ref, sem):
    copy = pltpu.make_async_copy(mask_hbm, mask_ref, sem)
    copy.start()
    copy.wait()


def sums_kernel(mask_hbm, values_ref, sums_ref, mask_ref, sem):
    tiles_c, tiles_r = mask_ref.shape
    load(mask_hbm, mask_ref, sem)
    for c in range(tiles_c):
        total = jnp.zeros((8, T), jnp.float32)
        for i in range(tiles_r):
            tile = values_ref[i * T:(i + 1) * T, c * T:(c + 1) * T].astype(jnp.float32)
            part = jnp.sum(tile.reshape(T // 8, 8, T), axis=0)
            total = total + jnp.where(mask_ref[c, i] != 0, part, 0.0)
        sums_ref[c:c + 1, :] = jnp.sum(total, axis=0, keepdims=True)


def column_sums(mask, values):
    return pl.pallas_call(
        sums_kernel,
        out_shape=pltpu.VMEM((mask.shape[0], T), jnp.float32),
        in_specs=[ANY, VMEM],
        out_specs=VMEM,
        scratch_shapes=[pltpu.SMEM(mask.shape, jnp.int32), pltpu.SemaphoreType.DMA],
        cost_estimate=pl.CostEstimate(flops=2**20, bytes_accessed=2 * 2**20, transcendentals=0),
        compiler_params=pltpu.CompilerParams(vmem_limit_bytes=GRANT),
        name="column_sums",
    )(mask, values)


def quarter_kernel(mask_hbm, values_ref, out_ref, mask_ref, sem):
    tiles_c, _ = mask_ref.shape
    load(mask_hbm, mask_ref, sem)
    layer = lax.axis_index("layer")
    first = ((layer & 1) * 2 + lax.div(layer, 2)) * tiles_c
    for i in range(out_ref.shape[0] // T):
        at = pl.ds(pl.multiple_of((first + i) * T, T), T)
        for c in range(tiles_c):
            tile = values_ref[at, c * T:(c + 1) * T]
            out_ref[i * T:(i + 1) * T, c * T:(c + 1) * T] = jnp.where(
                mask_ref[c, first + i] != 0, tile, jnp.zeros_like(tile))


def masked_quarter(mask, values, n_layer):
    height, width = values.shape
    return pl.pallas_call(
        quarter_kernel,
        out_shape=pltpu.VMEM((height // n_layer, width), jnp.bfloat16),
        in_specs=[ANY, VMEM],
        out_specs=VMEM,
        scratch_shapes=[pltpu.SMEM(mask.shape, jnp.int32), pltpu.SemaphoreType.DMA],
        cost_estimate=pl.CostEstimate(flops=2**18, bytes_accessed=2**20, transcendentals=0),
        compiler_params=pltpu.CompilerParams(vmem_limit_bytes=GRANT),
        name="masked_quarter",
    )(mask, values)


def scale_kernel(halves, per, raw_ref, mass_ref, part_ref):
    size = HEAD + per * T
    sums = mass_ref[...] / SCALE
    tiles_c = sums.shape[0]
    for h in range(halves):
        head = raw_ref[h * size:h * size + HEAD, :]
        part_ref[h * size:h * size + HEAD, :] = head
        which = lax.rem(head.astype(jnp.float32).astype(jnp.int32), tiles_c)
        for j in range(per):
            mine = which[j:j + 1, :]
            mass = sums[0:1, :]
            for c in range(1, tiles_c):
                mass = jnp.where(mine == c, sums[c:c + 1, :], mass)
            at = slice(h * size + HEAD + j * T, h * size + HEAD + (j + 1) * T)
            part_ref[at, :] = (raw_ref[at, :].astype(jnp.float32) / mass).astype(jnp.bfloat16)


def scale(raw, mass, per, halves):
    return pl.pallas_call(
        functools.partial(scale_kernel, halves, per),
        out_shape=pltpu.VMEM(raw.shape, raw.dtype),
        in_specs=[VMEM, VMEM],
        out_specs=VMEM,
        cost_estimate=pl.CostEstimate(flops=2**20, bytes_accessed=2**20, transcendentals=0),
        compiler_params=pltpu.CompilerParams(vmem_limit_bytes=GRANT),
        name="scale",
    )(raw, mass)


def product_kernel(n_parts, counts, per, again, *refs):
    part_refs = refs[:n_parts]
    if again:
        right_ref, _, out_ref = refs[n_parts:n_parts + 3]
    else:
        quarter_refs, (right_ref, out_ref) = refs[n_parts:-5], refs[-5:-3]
        for m, ref in enumerate(quarter_refs):
            height = ref.shape[0]
            right_ref[m * height:(m + 1) * height, :] = ref[...]
    spots, table, sem = refs[-3:]
    layer = lax.axis_index("layer")
    n_layer, rows, _ = out_ref.shape
    kt = right_ref.shape[0] // T
    chunks = [lax.rem(g + n_layer - layer, n_layer) for g in range(n_layer)]
    size = HEAD + per * T

    lane = lax.broadcasted_iota(jnp.int32, (8, T), 1)
    found = jnp.zeros((8, T), jnp.int32)
    q = 0
    for ref, count in zip(part_refs, counts, strict=True):
        for h in range(count):
            head = ref[h * size:h * size + HEAD, :].astype(jnp.float32).astype(jnp.int32)
            found = jnp.where(lane == q, head[:8, :], found)
            q += 1
    spots[...] = found
    if not again:
        def zero(i, _):
            out_ref[:, pl.ds(pl.multiple_of(i * T, T), T), :] = jnp.zeros((n_layer, T, T), jnp.float32)
            return 0

        lax.fori_loop(0, rows // T, zero, 0)
    copy = pltpu.make_async_copy(spots, table, sem)
    copy.start()
    copy.wait()
    q = 0
    for ref, count in zip(part_refs, counts, strict=True):
        for h in range(count):
            for j in range(per):
                t = table[j, q]
                at = pl.ds(pl.multiple_of(lax.div(t, kt) * T, T), T)
                rows_of = pl.ds(pl.multiple_of(lax.rem(t, kt) * T, T), T)
                tile = ref[h * size + HEAD + j * T:h * size + HEAD + (j + 1) * T, :]
                out = jnp.dot(tile, right_ref[rows_of, :], preferred_element_type=jnp.float32)
                for g, chunk in enumerate(chunks):
                    out_ref[chunk, at, :] += out[:, g * T:(g + 1) * T]
            q += 1


def product(parts, counts, per, rights, rows, n_layer, total=None):
    n_parts = len(parts)
    again = total is not None
    width = rights[0].shape[1]
    depth = sum(r.shape[0] for r in rights)
    tiles = sum(counts) * per
    result = pltpu.VMEM((n_layer, rows + T, width // n_layer), jnp.float32)
    right = pltpu.VMEM((depth, width), jnp.bfloat16)
    return pl.pallas_call(
        functools.partial(product_kernel, n_parts, counts, per, again),
        out_shape=result if again else (right, result),
        in_specs=[VMEM] * (n_parts + len(rights) + again),
        out_specs=VMEM if again else (VMEM, VMEM),
        scratch_shapes=[
            pltpu.VMEM((8, T), jnp.int32),
            pltpu.SMEM((8, T), jnp.int32),
            pltpu.SemaphoreType.DMA,
        ],
        input_output_aliases={n_parts + 1: 0} if again else {},
        cost_estimate=pl.CostEstimate(flops=2 * tiles * T * T * width, bytes_accessed=2**20, transcendentals=0),
        compiler_params=pltpu.CompilerParams(vmem_limit_bytes=GRANT),
        name="add_product" if again else "product",
    )(*parts, *rights, *((total,) if again else ()))


def coords(sizes):
    n_row, n_col, n_layer = sizes
    for r in range(n_row):
        for c in range(n_col):
            for y in range(n_layer):
                yield r, c, y


def flat(r, c, y, sizes):
    return (r * sizes[1] + c) * sizes[2] + y


def shards(sizes, values, tile_mask):
    n_row, n_col, n_layer = sizes
    axes = ("row", "col", "layer")
    height, _ = values.shape
    slots = tile_mask.size // 2
    halves = 2
    per = slots // n_layer // halves
    half = HEAD + per * T
    n_z = n_col // 2
    depth = height * n_row // n_layer
    f16, f32 = jnp.float16, jnp.float32

    mask = tile_mask.T
    hbm = functools.partial(pltpu.with_memory_space_constraint, memory_space=pltpu.HBM)
    raw = share(hbm(mask), hbm(values), per, halves, depth // T)

    spread = {}
    for r, c, y in coords(sizes):
        zz, hi = c // 2, c % 2
        y_to = hi * 2 + zz % 2
        move, core = {0: (1, 0), 1: (-1, 1), 2: (0, 0), 3: (0, 1)}[(y - y_to) % n_layer]
        spread[r, c, y] = flat(r // 2 * 2 + core, (zz + move) % n_z * 2 + r % 2, y_to, sizes)
    table = [(flat(*at, sizes), to) for at, to in spread.items()]
    raw = lax.ppermute(raw, axes, table)
    mass = lax.ppermute(lax.psum(column_sums(mask, values), "row"), axes, table)
    quarter = masked_quarter(mask, values, n_layer)
    part = scale(raw, mass, per, halves)

    def ring(step):
        return [(c, (c // 2 + step) % n_z * 2 + c % 2) for c in range(n_col)]

    swap = [(r, r ^ 1) for r in range(n_row)]
    last = n_z // 2
    mine = [part]
    up = down = part
    for step in range(1, last + 1):
        if step == last:
            up, down = up[:half], down[half:]
        up = lax.ppermute(up, "col", ring(1))
        down = lax.ppermute(down, "col", ring(-1))
        mine += [up, down]
    parts = [(p, lax.ppermute(p, "row", swap)) for p in mine]

    rights = []
    for m in range(n_row):
        perm = []
        for r, c, y in coords(sizes):
            lo, core, zz, hi = r // 2, r % 2, c // 2, c % 2
            lo_to, hi_to = lo ^ m // 2, core ^ m % 2
            to = (lo_to * 2 + (hi ^ hi_to ^ lo_to ^ 1), zz * 2 + hi_to, y)
            perm.append((flat(r, c, y, sizes), flat(*to, sizes)))
        rights.append(lax.ppermute(quarter, axes, perm))
    early = [p for pair in parts[:2 * last - 3] for p in pair]
    late = [p for pair in parts[2 * last - 3:] for p in pair]
    right, out = product(early, [p.shape[0] // half for p in early], per, rights, height, n_layer)
    out = product(late, [p.shape[0] // half for p in late], per, [right], height, n_layer, out)

    up = [(y, (y + 1) % n_layer) for y in range(n_layer)]
    down = [(y, (y - 1) % n_layer) for y in range(n_layer)]
    mid = height // 2
    send = lax.optimization_barrier(out[1:, :height].astype(f16))
    far_a = lax.ppermute(send[1, :mid], "layer", up)
    far_b = lax.ppermute(send[1, mid:], "layer", down)
    up_b = lax.ppermute(send[0, mid:], "layer", up)
    down_a = lax.ppermute(send[2, :mid], "layer", down)
    up_a = (out[1, :mid] + far_a.astype(f32)).astype(f16)
    down_b = (out[3, mid:height] + far_b.astype(f32)).astype(f16)
    up_a, down_b = lax.optimization_barrier((up_a, down_b))
    up_a = lax.ppermute(up_a, "layer", up)
    down_b = lax.ppermute(down_b, "layer", down)
    total = jnp.concatenate([
        out[0, :mid] + (up_a.astype(f32) + down_a.astype(f32)),
        out[0, mid:height] + (up_b.astype(f32) + down_b.astype(f32)),
    ]).astype(f16)

    owner = {}
    for r in range(n_row):
        for c in range(n_col):
            lo, core, hi = r // 2, r % 2, c % 2
            owner[r, c] = (lo * 2 + hi, c // 2 * 2 + (core ^ hi ^ lo ^ 1))
    expanded = lax.ppermute(
        total, ("row", "col"), [(r * n_col + c, o[0] * n_col + o[1]) for (r, c), o in owner.items()])
    summand = total.astype(f32)
    summand = jnp.sum(summand * summand, axis=0)
    weights = []
    for k in range(1, n_row):
        perm = [(r * n_col + c, (o[0] ^ k) * n_col + o[1]) for (r, c), o in owner.items()]
        weights.append(lax.ppermute(summand, ("row", "col"), perm))
    expanded = expanded.astype(f32)
    inflated = expanded * expanded
    weight = jnp.sum(inflated, axis=0) + (weights[0] + (weights[1] + weights[2]))
    order = height * n_row
    return order * 1.0 * inflated / weight[None, :]


def solution(mesh):
    sizes = tuple(mesh.shape[a] for a in ("row", "col", "layer"))

    def body(values, tile_mask):
        return shards(sizes, values, tile_mask)

    return jax.shard_map(
        body,
        mesh=mesh,
        in_specs=(P("row", "col"), P("row", "col")),
        out_specs=P("row", ("col", "layer")),
        check_vma=False,
    )
```

```python
import functools

import jax
import jax.numpy as jnp
from jax import lax
from jax.experimental import pallas as pl
from jax.experimental.pallas import tpu as pltpu
from jax.sharding import PartitionSpec as P


T = 128
HEAD = 16
SCALE = 16.0
GRANT = 16 * 2**20
VMEM = pl.BlockSpec(memory_space=pltpu.VMEM)
HBM = pl.BlockSpec(memory_space=pltpu.HBM)
ANY = pl.BlockSpec(memory_space=pl.ANY)


def share_kernel(halves, per, depth_tiles, mask_hbm, values_hbm, part_ref, mask_ref, table_ref, sem):
    tiles_c, tiles_r = mask_ref.shape
    layer, row, z = lax.axis_index("layer"), lax.axis_index("row"), lax.div(lax.axis_index("col"), 2)
    section = lax.div(z, 2) ^ row
    dead = tiles_r * tiles_c
    count = halves * per
    size = HEAD + per * T
    copy = pltpu.make_async_copy(mask_hbm, mask_ref, sem)
    copy.start()
    copy.wait()
    for s in range(count):
        table_ref[s] = dead
    n = -layer * count
    for i in range(tiles_r):
        for c in range(tiles_c):
            live = mask_ref[c, i] != 0
            spot = jnp.where(live & (n >= 0) & (n < count), n, count)
            table_ref[spot] = i * tiles_c + c
            n = n + live.astype(jnp.int32)
    starts = [(s // per) * size + HEAD + (s % per) * T for s in range(count)]

    def fetch(s):
        t = table_ref[s]
        i, c = lax.div(t, tiles_c), lax.rem(t, tiles_c)
        return pltpu.make_async_copy(
            values_hbm.at[pl.ds(pl.multiple_of(i * T, T), T), pl.ds(pl.multiple_of(c * T, T), T)],
            part_ref.at[starts[s]:starts[s] + T, :],
            sem,
        )

    for s in range(count):
        @pl.when(table_ref[s] < dead)
        def _():
            fetch(s).start()

        @pl.when(table_ref[s] >= dead)
        def _():
            part_ref[starts[s]:starts[s] + T, :] = jnp.zeros((T, T), jnp.bfloat16)

    row = lax.broadcasted_iota(jnp.int32, (HEAD, T), 0)
    for h in range(halves):
        head = jnp.full((HEAD, T), tiles_r * depth_tiles, jnp.int32)
        for j in range(per):
            t = table_ref[h * per + j]
            at = lax.div(t, tiles_c) * depth_tiles + section * tiles_c + lax.rem(t, tiles_c)
            head = jnp.where((row == j) & (t < dead), at, head)
        part_ref[h * size:h * size + HEAD, :] = head.astype(jnp.float32).astype(jnp.bfloat16)
    for s in range(count):
        @pl.when(table_ref[s] < dead)
        def _():
            fetch(s).wait()


def share(mask, values, per, halves, depth_tiles):
    return pl.pallas_call(
        functools.partial(share_kernel, halves, per, depth_tiles),
        out_shape=pltpu.VMEM((halves * (HEAD + per * T), T), jnp.bfloat16),
        in_specs=[HBM, HBM],
        out_specs=VMEM,
        scratch_shapes=[
            pltpu.SMEM(mask.shape, jnp.int32),
            pltpu.SMEM((halves * per + 1,), jnp.int32),
            pltpu.SemaphoreType.DMA,
        ],
        cost_estimate=pl.CostEstimate(flops=2**20, bytes_accessed=2 * 2**20, transcendentals=0),
        compiler_params=pltpu.CompilerParams(vmem_limit_bytes=GRANT),
        name="share",
    )(mask, values)


def load(mask_hbm, mask_ref, sem):
    copy = pltpu.make_async_copy(mask_hbm, mask_ref, sem)
    copy.start()
    copy.wait()


def sums_kernel(mask_hbm, values_ref, sums_ref, mask_ref, sem):
    tiles_c, tiles_r = mask_ref.shape
    load(mask_hbm, mask_ref, sem)
    for c in range(tiles_c):
        total = jnp.zeros((8, T), jnp.float32)
        for i in range(tiles_r):
            tile = values_ref[i * T:(i + 1) * T, c * T:(c + 1) * T].astype(jnp.float32)
            part = jnp.sum(tile.reshape(T // 8, 8, T), axis=0)
            total = total + jnp.where(mask_ref[c, i] != 0, part, 0.0)
        sums_ref[c:c + 1, :] = jnp.sum(total, axis=0, keepdims=True)


def column_sums(mask, values):
    return pl.pallas_call(
        sums_kernel,
        out_shape=pltpu.VMEM((mask.shape[0], T), jnp.float32),
        in_specs=[ANY, VMEM],
        out_specs=VMEM,
        scratch_shapes=[pltpu.SMEM(mask.shape, jnp.int32), pltpu.SemaphoreType.DMA],
        cost_estimate=pl.CostEstimate(flops=2**20, bytes_accessed=2 * 2**20, transcendentals=0),
        compiler_params=pltpu.CompilerParams(vmem_limit_bytes=GRANT),
        name="column_sums",
    )(mask, values)


def quarter_kernel(mask_hbm, values_ref, out_ref, mask_ref, sem):
    tiles_c, _ = mask_ref.shape
    load(mask_hbm, mask_ref, sem)
    layer = lax.axis_index("layer")
    first = ((layer & 1) * 2 + lax.div(layer, 2)) * tiles_c
    for i in range(out_ref.shape[0] // T):
        at = pl.ds(pl.multiple_of((first + i) * T, T), T)
        for c in range(tiles_c):
            tile = values_ref[at, c * T:(c + 1) * T]
            out_ref[i * T:(i + 1) * T, c * T:(c + 1) * T] = jnp.where(
                mask_ref[c, first + i] != 0, tile, jnp.zeros_like(tile))


def masked_quarter(mask, values, n_layer):
    height, width = values.shape
    return pl.pallas_call(
        quarter_kernel,
        out_shape=pltpu.VMEM((height // n_layer, width), jnp.bfloat16),
        in_specs=[ANY, VMEM],
        out_specs=VMEM,
        scratch_shapes=[pltpu.SMEM(mask.shape, jnp.int32), pltpu.SemaphoreType.DMA],
        cost_estimate=pl.CostEstimate(flops=2**18, bytes_accessed=2**20, transcendentals=0),
        compiler_params=pltpu.CompilerParams(vmem_limit_bytes=GRANT),
        name="masked_quarter",
    )(mask, values)


def scale_kernel(halves, per, raw_ref, mass_ref, part_ref):
    size = HEAD + per * T
    sums = mass_ref[...] / SCALE
    tiles_c = sums.shape[0]
    for h in range(halves):
        head = raw_ref[h * size:h * size + HEAD, :]
        part_ref[h * size:h * size + HEAD, :] = head
        which = lax.rem(head.astype(jnp.float32).astype(jnp.int32), tiles_c)
        for j in range(per):
            mine = which[j:j + 1, :]
            mass = sums[0:1, :]
            for c in range(1, tiles_c):
                mass = jnp.where(mine == c, sums[c:c + 1, :], mass)
            at = slice(h * size + HEAD + j * T, h * size + HEAD + (j + 1) * T)
            part_ref[at, :] = (raw_ref[at, :].astype(jnp.float32) / mass).astype(jnp.bfloat16)


def scale(raw, mass, per, halves):
    return pl.pallas_call(
        functools.partial(scale_kernel, halves, per),
        out_shape=pltpu.VMEM(raw.shape, raw.dtype),
        in_specs=[VMEM, VMEM],
        out_specs=VMEM,
        cost_estimate=pl.CostEstimate(flops=2**20, bytes_accessed=2**20, transcendentals=0),
        compiler_params=pltpu.CompilerParams(vmem_limit_bytes=GRANT),
        name="scale",
    )(raw, mass)


def product_kernel(n_parts, counts, per, again, *refs):
    part_refs = refs[:n_parts]
    if again:
        right_ref, _, out_ref = refs[n_parts:n_parts + 3]
    else:
        quarter_refs, (right_ref, out_ref) = refs[n_parts:-5], refs[-5:-3]
        for m, ref in enumerate(quarter_refs):
            height = ref.shape[0]
            right_ref[m * height:(m + 1) * height, :] = ref[...]
    spots, table, sem = refs[-3:]
    layer = lax.axis_index("layer")
    n_layer, rows, _ = out_ref.shape
    kt = right_ref.shape[0] // T
    chunks = [lax.rem(g + n_layer - layer, n_layer) for g in range(n_layer)]
    size = HEAD + per * T

    lane = lax.broadcasted_iota(jnp.int32, (8, T), 1)
    found = jnp.zeros((8, T), jnp.int32)
    q = 0
    for ref, count in zip(part_refs, counts, strict=True):
        for h in range(count):
            head = ref[h * size:h * size + HEAD, :].astype(jnp.float32).astype(jnp.int32)
            found = jnp.where(lane == q, head[:8, :], found)
            q += 1
    spots[...] = found
    if not again:
        def zero(i, _):
            out_ref[:, pl.ds(pl.multiple_of(i * T, T), T), :] = jnp.zeros((n_layer, T, T), jnp.float32)
            return 0

        lax.fori_loop(0, rows // T, zero, 0)
    copy = pltpu.make_async_copy(spots, table, sem)
    copy.start()
    copy.wait()
    q = 0
    for ref, count in zip(part_refs, counts, strict=True):
        for h in range(count):
            for j in range(per):
                t = table[j, q]
                at = pl.ds(pl.multiple_of(lax.div(t, kt) * T, T), T)
                rows_of = pl.ds(pl.multiple_of(lax.rem(t, kt) * T, T), T)
                tile = ref[h * size + HEAD + j * T:h * size + HEAD + (j + 1) * T, :]
                out = jnp.dot(tile, right_ref[rows_of, :], preferred_element_type=jnp.float32)
                for g, chunk in enumerate(chunks):
                    out_ref[chunk, at, :] += out[:, g * T:(g + 1) * T]
            q += 1


def product(parts, counts, per, rights, rows, n_layer, total=None):
    n_parts = len(parts)
    again = total is not None
    width = rights[0].shape[1]
    depth = sum(r.shape[0] for r in rights)
    tiles = sum(counts) * per
    result = pltpu.VMEM((n_layer, rows + T, width // n_layer), jnp.float32)
    right = pltpu.VMEM((depth, width), jnp.bfloat16)
    return pl.pallas_call(
        functools.partial(product_kernel, n_parts, counts, per, again),
        out_shape=result if again else (right, result),
        in_specs=[VMEM] * (n_parts + len(rights) + again),
        out_specs=VMEM if again else (VMEM, VMEM),
        scratch_shapes=[
            pltpu.VMEM((8, T), jnp.int32),
            pltpu.SMEM((8, T), jnp.int32),
            pltpu.SemaphoreType.DMA,
        ],
        input_output_aliases={n_parts + 1: 0} if again else {},
        cost_estimate=pl.CostEstimate(flops=2 * tiles * T * T * width, bytes_accessed=2**20, transcendentals=0),
        compiler_params=pltpu.CompilerParams(vmem_limit_bytes=GRANT),
        name="add_product" if again else "product",
    )(*parts, *rights, *((total,) if again else ()))


def coords(sizes):
    n_row, n_col, n_layer = sizes
    for r in range(n_row):
        for c in range(n_col):
            for y in range(n_layer):
                yield r, c, y


def flat(r, c, y, sizes):
    return (r * sizes[1] + c) * sizes[2] + y


def named(array, axes, perm):
    return lax.ppermute(array, axes, perm)


def shards(sizes, values, tile_mask):
    n_row, n_col, n_layer = sizes
    axes = ("row", "col", "layer")
    height, _ = values.shape
    slots = tile_mask.size // 2
    halves = 2
    per = slots // n_layer // halves
    half = HEAD + per * T
    n_z = n_col // 2
    depth = height * n_row // n_layer
    f16, f32 = jnp.float16, jnp.float32

    mask = tile_mask.T
    hbm = functools.partial(pltpu.with_memory_space_constraint, memory_space=pltpu.HBM)
    raw = share(hbm(mask), hbm(values), per, halves, depth // T)

    spread = {}
    for r, c, y in coords(sizes):
        zz, hi = c // 2, c % 2
        y_to = hi * 2 + zz % 2
        move, core = {0: (1, 0), 1: (-1, 1), 2: (0, 0), 3: (0, 1)}[(y - y_to) % n_layer]
        spread[r, c, y] = flat(r // 2 * 2 + core, (zz + move) % n_z * 2 + r % 2, y_to, sizes)
    table = [(flat(*at, sizes), to) for at, to in spread.items()]
    raw = named(raw, axes, table)
    sums = column_sums(mask, values)
    others = [named(sums, "row", [(r, r ^ k) for r in range(n_row)]) for k in range(1, n_row)]
    mass = named((sums + others[0]) + (others[1] + others[2]), axes, table)
    quarter = masked_quarter(mask, values, n_layer)
    part = scale(raw, mass, per, halves)

    def ring(step):
        return [(c, (c // 2 + step) % n_z * 2 + c % 2) for c in range(n_col)]

    swap = [(r, r ^ 1) for r in range(n_row)]
    last = n_z // 2
    mine = [part]
    up = down = part
    for step in range(1, last + 1):
        if step == last:
            up, down = up[:half], down[half:]
        up = named(up, "col", ring(1))
        down = named(down, "col", ring(-1))
        mine += [up, down]
    parts = [(p, named(p, "row", swap)) for p in mine]

    rights = []
    for m in range(n_row):
        perm = []
        for r, c, y in coords(sizes):
            lo, core, zz, hi = r // 2, r % 2, c // 2, c % 2
            lo_to, hi_to = lo ^ m // 2, core ^ m % 2
            to = (lo_to * 2 + (hi ^ hi_to ^ lo_to ^ 1), zz * 2 + hi_to, y)
            perm.append((flat(r, c, y, sizes), flat(*to, sizes)))
        rights.append(named(quarter, axes, perm))
    early = [p for pair in parts[:2 * last - 3] for p in pair]
    late = [p for pair in parts[2 * last - 3:] for p in pair]
    right, out = product(early, [p.shape[0] // half for p in early], per, rights, height, n_layer)
    out = product(late, [p.shape[0] // half for p in late], per, [right], height, n_layer, out)

    up = [(y, (y + 1) % n_layer) for y in range(n_layer)]
    down = [(y, (y - 1) % n_layer) for y in range(n_layer)]
    mid = height // 2
    send = lax.optimization_barrier(out[1:, :height].astype(f16))
    far_a = named(send[1, :mid], "layer", up)
    far_b = named(send[1, mid:], "layer", down)
    up_b = named(send[0, mid:], "layer", up)
    down_a = named(send[2, :mid], "layer", down)
    up_a = (out[1, :mid] + far_a.astype(f32)).astype(f16)
    down_b = (out[3, mid:height] + far_b.astype(f32)).astype(f16)
    up_a, down_b = lax.optimization_barrier((up_a, down_b))
    up_a = named(up_a, "layer", up)
    down_b = named(down_b, "layer", down)
    total = jnp.concatenate([
        out[0, :mid] + (up_a.astype(f32) + down_a.astype(f32)),
        out[0, mid:height] + (up_b.astype(f32) + down_b.astype(f32)),
    ]).astype(f16)

    owner = {}
    for r in range(n_row):
        for c in range(n_col):
            lo, core, hi = r // 2, r % 2, c % 2
            owner[r, c] = (lo * 2 + hi, c // 2 * 2 + (core ^ hi ^ lo ^ 1))
    expanded = named(
        total, ("row", "col"), [(r * n_col + c, o[0] * n_col + o[1]) for (r, c), o in owner.items()])
    summand = total.astype(f32)
    summand = jnp.sum(summand * summand, axis=0)
    weights = []
    for k in range(1, n_row):
        perm = [(r * n_col + c, (o[0] ^ k) * n_col + o[1]) for (r, c), o in owner.items()]
        weights.append(named(summand, ("row", "col"), perm))
    expanded = expanded.astype(f32)
    inflated = expanded * expanded
    weight = jnp.sum(inflated, axis=0) + (weights[0] + (weights[1] + weights[2]))
    order = height * n_row
    return order * 1.0 * inflated / weight[None, :]


def solution(mesh):
    sizes = tuple(mesh.shape[a] for a in ("row", "col", "layer"))

    def body(values, tile_mask):
        return shards(sizes, values, tile_mask)

    return jax.shard_map(
        body,
        mesh=mesh,
        in_specs=(P("row", "col"), P("row", "col")),
        out_specs=P("row", ("col", "layer")),
        check_vma=False,
    )
```
